32 devices in a mesh: rad: 4 (over y, x), azi: 8 (over z, core).
Axes of the slice: x: 2, y: 2, z: 4, core: 2. Of those that a mesh axis runs over, the one named last changes fastest.
Arguments:
- blocks: float32 [512, 8, 4096], P(('rad', 'azi')), may hold values from -8 to 8
- assignment: int32 [512], replicated, may hold values from 0 to 511, as said below
- levels: int32 [512], P(('rad', 'azi')), may hold values from 0 to 2
- coupling: float32 [3, 8, 8], replicated, may hold values from -2 to 2
- damping: float32 [8], replicated, may hold values from 0.5 to 5
Outputs:
- new_blocks: float32 [512, 8, 4096], P(('rad', 'azi'))
- tendency: float32 [512, 8, 4096], P(('rad', 'azi'))
The draws below stay inside these ranges and needn't reach their ends.
Inputs may be any that keep to these rules, and one draw needn't show every extreme that they name: A permutation. The slot assignment[i] lies on a device (slot // 16, devices ordered rad then azi) with the same rad index as the device that holds block i now. From one device to one device (itself included) go at most 2 blocks, and every device sends exactly 2 blocks to some one device.
All inputs are finite; a program needn't handle non-finite values.
Results may differ from the reference program's by a relative error of at most 0.0003.
Values sent between devices are 32-bit elements; how exact they have to be, the bound alone decides.
No kernel may reach another device: no remote copies, remote signals or barrier semaphores. Data moves between devices by JAX's collectives and lax.ppermute only.
A program may use at most 128 MiB of HBM per device.

```python
import math
import jax
import jax.numpy as jnp
from jax import lax

EDGE = 16
CHANNELS = 8
BLOCKS_DEV = 16
CAPACITY = 2
MESHBLOCKS = 512
RAD_CELLS = 64
AZI_CELLS = 128
VERT_CELLS = 256
N_RAD = 4
N_AZI = 8


def placement_table(seed_key):

    def one_row(row_index):
        row_key = jax.random.fold_in(seed_key, row_index)
        block_ids = jnp.arange(BLOCKS_DEV)
        offset_base = jnp.where(block_ids < CAPACITY, 0, 1 + (block_ids - CAPACITY) % (N_AZI - 1))
        relabel = jax.random.permutation(jax.random.fold_in(row_key, 1), N_AZI)

        def one_source(source):
            shuffled = jax.random.permutation(jax.random.fold_in(row_key, 100 + source), BLOCKS_DEV)
            return (source + relabel[offset_base[shuffled]]) % N_AZI
        target = jax.vmap(one_source)(jnp.arange(N_AZI)).reshape(-1)
        flat_ids = jnp.arange(N_AZI * BLOCKS_DEV)
        earlier = (target[:, None] == target[None, :]) & (flat_ids[None, :] < flat_ids[:, None])
        arrival_rank = jnp.sum(earlier.astype(jnp.int32), axis=1)

        def one_dest(dest_index):
            return jax.random.permutation(jax.random.fold_in(row_key, 1000 + dest_index), BLOCKS_DEV)
        shuffles = jax.vmap(one_dest)(jnp.arange(N_AZI))
        position = shuffles[target, arrival_rank]
        return (row_index * N_AZI + target) * BLOCKS_DEV + position
    return jax.vmap(one_row)(jnp.arange(N_RAD)).reshape(-1).astype(jnp.int32)


def level_table(seed_key):
    return jax.random.randint(jax.random.fold_in(seed_key, 21), (MESHBLOCKS,), 0, 3).astype(jnp.int32)


def channel_vector(flags):
    return flags.astype(jnp.float32).reshape(1, 1, 1, CHANNELS, 1, 1, 1)


def draw_assignment(key, part):
    return placement_table(jax.random.fold_in(key, 7))


def draw_levels(key, part):
    return level_table(key)


def draw_blocks(key, part):
    slot_table = placement_table(jax.random.fold_in(key, 7))
    full_shape = (N_RAD, N_AZI, BLOCKS_DEV, CHANNELS, EDGE, EDGE, EDGE)
    column_shape = (N_RAD, 1, BLOCKS_DEV, CHANNELS, EDGE, 1, EDGE)
    level_grid = level_table(key).astype(jnp.float32).reshape(N_RAD, N_AZI, BLOCKS_DEV, 1, 1, 1, 1) - 1.0
    cell_ids = jnp.arange(EDGE).astype(jnp.float32)
    azi_ramp = ((2.0 * cell_ids + 1.0) / EDGE - 1.0).reshape(1, 1, 1, 1, 1, EDGE, 1)
    level_part = level_grid * (1.0 + azi_ramp)
    channel_ids = jnp.arange(CHANNELS)
    channel_order = jax.random.permutation(jax.random.fold_in(key, 31), CHANNELS)
    mean_flag = channel_ids == 2
    tied_flag = (channel_order < CHANNELS // 2) & jnp.logical_not(mean_flag)
    column_flag = jnp.logical_not(tied_flag | mean_flag)
    mean_weight = channel_vector(mean_flag)
    tied_weight = channel_vector(tied_flag)
    column_weight = channel_vector(column_flag)
    rough_part = 0.25 * jnp.clip(jax.random.normal(jax.random.fold_in(key, 11), full_shape, jnp.float32), -2.5, 2.5)
    column_part = jax.random.uniform(jax.random.fold_in(key, 12), column_shape, jnp.float32, -1.0, 1.0)
    column_scale = 3.5 * column_weight + tied_weight + 0.3 * mean_weight
    tied_scale = 3.0 * tied_weight + 1.5 * mean_weight
    mean_base = 3.8 * mean_weight
    azi_where = (jnp.arange(N_AZI)[:, None] * EDGE + jnp.arange(EDGE)[None, :]).astype(jnp.float32) / (EDGE * N_AZI)
    azi_weight = (0.5 + azi_where).reshape(1, N_AZI, 1, 1, 1, EDGE, 1)
    slot_field = azi_weight * rough_part + column_scale * column_part
    slot_field = slot_field + tied_scale * level_part + mean_base
    slot_field = slot_field.reshape(MESHBLOCKS, CHANNELS, EDGE * EDGE * EDGE)
    return jnp.take(slot_field, slot_table, axis=0)


def shard_levels(rng, shape, pieces, least, largest):
    def one(axis_at, blocks):
        steps = jax.random.uniform(jax.random.fold_in(jax.random.fold_in(rng, 6), axis_at), (blocks,), jnp.float32, least / len(pieces), largest / len(pieces))
        return jnp.repeat(jnp.exp(steps), shape[axis_at] // blocks).reshape((-1,) + (1,) * (len(shape) - axis_at - 1))

    loudness = one(*pieces[0])
    for cut in pieces[1:]:
        loudness = loudness * one(*cut)
    return loudness


def centred(stream_key, shape, deviation, reach, kind=jnp.bfloat16):
    values = deviation * jax.random.normal(stream_key, shape, jnp.float32)
    return jnp.clip(values, min=-reach, max=reach).astype(kind)


def setup_inputs(seed: int = 0) -> dict:
    seeds = jax.random.split(jax.random.key(seed), 6)
    blocks = draw_blocks(jax.random.fold_in(seeds[5], 71), 0)
    assignment = draw_assignment(jax.random.fold_in(seeds[5], 71), 0)
    levels = draw_levels(jax.random.fold_in(seeds[5], 71), 0)
    coupling = centred(seeds[3], (3, CHANNELS, CHANNELS), CHANNELS ** -0.5, 2.0, jnp.float32)
    damping = jnp.clip(jnp.exp(jax.random.uniform(seeds[4], (CHANNELS,), jnp.float32, math.log(0.5), math.log(5.0))), 0.5, 5.0)
    return dict(blocks=blocks, assignment=assignment, levels=levels, coupling=coupling, damping=damping)


time_step = 0.02
signal_speed = 2.0
shear_rate = -1.5


def limited(lower, upper):
    return jnp.where(lower * upper > 0.0, jnp.sign(lower) * jnp.minimum(jnp.abs(lower), jnp.abs(upper)), 0.0)


def window(array, offset, length, along):
    return lax.slice_in_dim(array, offset, offset + length, axis=along)


def flux_change(padded, along, velocity, signal, matrix):
    inner = padded.shape[along] - 4
    differences = window(padded, 1, inner + 3, along) - window(padded, 0, inner + 3, along)
    slopes = limited(window(differences, 0, inner + 2, along), window(differences, 1, inner + 2, along))
    left_state = window(padded, 1, inner + 1, along) + 0.5 * window(slopes, 0, inner + 1, along)
    right_state = window(padded, 2, inner + 1, along) - 0.5 * window(slopes, 1, inner + 1, along)
    summed = left_state + right_state
    mixed_flux = jnp.einsum("ce,e...->c...", matrix, summed, precision=lax.Precision.HIGHEST)
    face_values = 0.5 * mixed_flux - 0.5 * signal * (right_state - left_state)
    if velocity is not None:
        face_values = face_values + 0.5 * velocity * summed
    return window(face_values, 1, inner, along) - window(face_values, 0, inner, along)


def increment(state_field, padded_rad, padded_azi, column_mean, step_ratio, shear_speed, coupling, damping):
    padded_vert = jnp.concatenate([state_field[..., -2:], state_field, state_field[..., :2]], axis=3)
    velocity = (shear_speed[:, None] + column_mean[2])[:, None, :]
    signal = jnp.abs(velocity) + signal_speed
    total_change = flux_change(padded_rad, 1, None, signal_speed, coupling[0])
    total_change = total_change + flux_change(padded_azi, 2, velocity, signal, coupling[1])
    total_change = total_change + flux_change(padded_vert, 3, None, signal_speed, coupling[2])
    relax = time_step * damping[:, None, None, None] * (state_field - column_mean[:, :, None, :])
    return -step_ratio * total_change - relax


def reference(blocks, assignment, levels, coupling, damping):
    migrated = jnp.zeros_like(blocks).at[assignment].set(blocks)
    shaped = migrated.reshape(N_RAD, N_AZI, BLOCKS_DEV, CHANNELS, EDGE, EDGE, EDGE)
    start_field = shaped.transpose(3, 0, 4, 1, 5, 2, 6).reshape(CHANNELS, RAD_CELLS, AZI_CELLS, VERT_CELLS)
    factor = jnp.where(levels == 0, 1.0, jnp.where(levels == 1, 2.0, 4.0)).astype(jnp.float32) * time_step
    factor = factor.reshape(N_RAD, N_AZI, BLOCKS_DEV)
    step_ratio = jnp.repeat(jnp.repeat(jnp.repeat(factor, EDGE, axis=0), EDGE, axis=1), EDGE, axis=2)
    coords = (jnp.arange(RAD_CELLS).astype(jnp.float32) + 0.5) * (2.0 / RAD_CELLS) - 1.0
    shear_speed = shear_rate * coords

    def advance(state_field):
        column_mean = jnp.sum(state_field, axis=2) / AZI_CELLS
        padded_rad = jnp.pad(state_field, ((0, 0), (2, 2), (0, 0), (0, 0)))
        padded_azi = jnp.pad(state_field, ((0, 0), (0, 0), (2, 2), (0, 0)), mode="wrap")
        return increment(state_field, padded_rad, padded_azi, column_mean, step_ratio, shear_speed, coupling, damping)

    first_state = start_field + advance(start_field)
    final_state = 0.5 * start_field + 0.5 * (first_state + advance(first_state))
    tendency_grid = (final_state - start_field) / time_step

    def to_blocks(grid_field):
        split_field = grid_field.reshape(CHANNELS, N_RAD, EDGE, N_AZI, EDGE, BLOCKS_DEV, EDGE)
        return split_field.transpose(1, 3, 5, 0, 2, 4, 6).reshape(MESHBLOCKS, CHANNELS, EDGE * EDGE * EDGE)

    return to_blocks(final_state), to_blocks(tendency_grid)
```

```python
import functools

import jax
import jax.numpy as jnp
from jax import lax
from jax.experimental import pallas as pl
from jax.experimental.pallas import tpu as pltpu
from jax.sharding import PartitionSpec as P

EDGE = 16
CHANNELS = 8
CAPACITY = 2
LANES = 128

time_step = 0.02
signal_speed = 2.0
shear_rate = -1.5

ANY = pl.BlockSpec(memory_space=pl.ANY)
SMEM = pl.BlockSpec(memory_space=pltpu.SMEM)
VMEM = pl.BlockSpec(memory_space=pltpu.VMEM)
F32 = jnp.float32


def minmod(a, b):
    return jnp.maximum(jnp.minimum(a, b), jnp.minimum(jnp.maximum(a, b), 0.0))


def lane_group():
    return lax.broadcasted_iota(jnp.int32, (CHANNELS, LANES), 1) // EDGE


def swap_groups(rows, group):
    rows = list(rows)
    for bit in (1, 2, 4):
        low = (group & bit) == 0
        shift = EDGE * bit
        for i in range(8):
            if i & bit:
                continue
            a, b = rows[i], rows[i + bit]
            rows[i] = jnp.where(low, a, pltpu.roll(b, shift, 1))
            rows[i + bit] = jnp.where(low, pltpu.roll(a, LANES - shift, 1), b)
    return rows


def pack_kernel(azi_count, block_count, place, assignment, blocks, *refs):
    outs = refs[: azi_count - 1]
    table, fill, sems = refs[azi_count - 1 :]
    azi = place[0]
    first = place[1]
    for i in range(azi_count):
        fill[i] = 0
    for i in range(azi_count * CAPACITY):
        table[i] = 0

    def note(j, carry):
        device = lax.div(assignment[first + j], block_count)
        shift = lax.rem(lax.rem(device, azi_count) - azi + azi_count, azi_count)
        k = fill[shift]
        table[shift * CAPACITY + k] = j
        fill[shift] = k + 1
        return carry

    lax.fori_loop(0, block_count, note, 0)
    copies = []
    for shift in range(1, azi_count):
        for k in range(CAPACITY):
            spot = shift * CAPACITY + k
            copy = pltpu.make_async_copy(
                blocks.at[table[spot]], outs[shift - 1].at[k], sems.at[spot]
            )
            copy.start()
            copies.append(copy)
    for copy in copies:
        copy.wait()


def pack(place, assignment, blocks, azi_count):
    shape = (CAPACITY,) + blocks.shape[1:]
    spots = azi_count * CAPACITY
    return pl.pallas_call(
        functools.partial(pack_kernel, azi_count, blocks.shape[0]),
        out_shape=[jax.ShapeDtypeStruct(shape, F32)] * (azi_count - 1),
        in_specs=[SMEM, SMEM, ANY],
        out_specs=[ANY] * (azi_count - 1),
        scratch_shapes=[
            pltpu.SMEM((spots,), jnp.int32),
            pltpu.SMEM((azi_count,), jnp.int32),
            pltpu.SemaphoreType.DMA((spots,)),
        ],
        name="pack",
    )(place, assignment, blocks)


def column_kernel(azi_count, block_count, place, assignment, blocks, sums, table, fill):
    azi = place[0]
    first = place[1]
    row_first = place[2]
    own = place[3]
    group = lane_group()
    sums[...] = jnp.zeros(sums.shape, F32)

    def one(j, carry):
        slot = lax.rem(assignment[first + j], block_count)
        here = group == lax.rem(slot, 8)
        lanes = pl.ds(pl.multiple_of(lax.div(slot, 8) * LANES, LANES), LANES)
        for x in range(EDGE):
            base = x * EDGE * EDGE
            part = blocks[j, :, base : base + LANES] + blocks[j, :, base + LANES : base + 2 * LANES]
            for shift in (64, 32, 16):
                part = part + pltpu.roll(part, shift, 1)
            sums[x, :, lanes] = sums[x, :, lanes] + jnp.where(here, part, 0.0)
        return carry

    lax.fori_loop(0, block_count, one, 0)

    spots = azi_count * CAPACITY
    for i in range(spots):
        table[i] = -1
    for i in range(CAPACITY):
        table[spots + i] = 0

    def source(s, carry):
        shift = lax.rem(azi - s + azi_count, azi_count)
        fill[0] = 0

        def entry(j, inner):
            slot = assignment[row_first + s * block_count + j]

            @pl.when(lax.div(slot, block_count) == own)
            def _():
                k = fill[0]
                table[shift * CAPACITY + k] = lax.rem(slot, block_count)

                @pl.when(shift == 0)
                def _():
                    table[spots + k] = j

                fill[0] = k + 1

            return inner

        lax.fori_loop(0, block_count, entry, 0)
        return carry

    lax.fori_loop(0, azi_count, source, 0)


def column_sums(place, assignment, blocks, azi_count):
    block_count = blocks.shape[0]
    spots = azi_count * CAPACITY
    return pl.pallas_call(
        functools.partial(column_kernel, azi_count, block_count),
        out_shape=[
            jax.ShapeDtypeStruct((EDGE, CHANNELS, block_count * EDGE), F32),
            jax.ShapeDtypeStruct((spots + CAPACITY,), jnp.int32),
        ],
        in_specs=[SMEM, SMEM, VMEM],
        out_specs=[VMEM, SMEM],
        scratch_shapes=[pltpu.SMEM((1,), jnp.int32)],
        name="column_sums",
    )(place, assignment, blocks)


def unpack_kernel(azi_count, block_count, table, blocks, *refs):
    arrived = refs[: azi_count - 1]
    field, rad_head, rad_tail, azi_head, azi_tail, held, sems = refs[azi_count - 1 :]
    spots = azi_count * CAPACITY

    def copy_of(shift, k):
        spot = shift * CAPACITY + k
        if shift == 0:
            source = blocks.at[table[spots + k]]
        else:
            source = arrived[shift - 1].at[k]
        return pltpu.make_async_copy(source, held.at[jnp.maximum(table[spot], 0)], sems.at[spot])

    for shift in range(azi_count):
        for k in range(CAPACITY):

            @pl.when(table[shift * CAPACITY + k] >= 0)
            def _(shift=shift, k=k):
                copy_of(shift, k).start()

    for shift in range(azi_count):
        for k in range(CAPACITY):

            @pl.when(table[shift * CAPACITY + k] >= 0)
            def _(shift=shift, k=k):
                copy_of(shift, k).wait()

    group = lane_group()

    def row(x, carry):
        base = x * (EDGE * EDGE)
        for half in range(block_count // 8):
            lanes = slice(half * LANES, (half + 1) * LANES)
            for upper in range(2):
                at = pl.ds(pl.multiple_of(base + upper * LANES, LANES), LANES)
                tiles = swap_groups([held[half * 8 + i, :, at] for i in range(8)], group)
                for i in range(8):
                    field[x, upper * 8 + i, :, lanes] = tiles[i]
                for i in range(2):
                    if upper == 0:
                        azi_head[x, i, :, lanes] = tiles[i]
                    else:
                        azi_tail[x, i, :, lanes] = tiles[6 + i]
        return carry

    lax.fori_loop(0, EDGE, row, 0)
    rad_head[...] = field[0:2]
    rad_tail[...] = field[EDGE - 2 : EDGE]


def field_shapes(vertical):
    rad = jax.ShapeDtypeStruct((2, EDGE, CHANNELS, vertical), F32)
    azi = jax.ShapeDtypeStruct((EDGE, 2, CHANNELS, vertical), F32)
    return [jax.ShapeDtypeStruct((EDGE, EDGE, CHANNELS, vertical), F32), rad, rad, azi, azi]


def unpack(table, blocks, arrived, azi_count):
    block_count = blocks.shape[0]
    return pl.pallas_call(
        functools.partial(unpack_kernel, azi_count, block_count),
        out_shape=field_shapes(block_count * EDGE),
        in_specs=[SMEM] + [ANY] * azi_count,
        out_specs=[VMEM] * 5,
        scratch_shapes=[
            pltpu.VMEM(blocks.shape, F32),
            pltpu.SemaphoreType.DMA((azi_count * CAPACITY,)),
        ],
        name="unpack",
    )(table, blocks, *arrived)


def stage_row(x, padded, mixed, total, weights, mean, shear, finish):
    vertical = padded.shape[-1]
    velocity = jnp.broadcast_to(mean[x, 2:3, :], (CHANNELS, vertical)) + shear[x]
    half_velocity = 0.5 * velocity
    half_signal = 0.5 * jnp.abs(velocity) + 0.5 * signal_speed
    here = x + 2
    u = [padded[here, i] for i in range(4)]
    d = [u[i + 1] - u[i] for i in range(3)]
    s = [minmod(d[0], d[1]), minmod(d[1], d[2])]
    u1, u2, u3 = u[1:]
    d1, d2 = d[1:]
    s0, s1 = s
    for y in range(EDGE):
        u4 = padded[here, y + 4]
        d3 = u4 - u3
        s2 = minmod(d2, d3)
        sum_azi = (d1 + d2) + s1 - 0.5 * (s0 + s2)
        jump_azi = (d2 - d1) - 0.5 * (s2 - s0)
        cell = u2
        r0, r1, r3, r4 = (padded[here + k, y + 2] for k in (-2, -1, 1, 2))
        e0, e1, e2, e3 = r1 - r0, cell - r1, r3 - cell, r4 - r3
        t0, t1, t2 = minmod(e0, e1), minmod(e1, e2), minmod(e2, e3)
        sum_rad = (e1 + e2) + t1 - 0.5 * (t0 + t2)
        jump = (e2 - e1) - 0.5 * (t2 - t0)
        f1 = pltpu.roll(cell, vertical - 1, 1) - cell
        f0 = pltpu.roll(f1, 1, 1)
        g1 = minmod(f0, f1)
        g0 = pltpu.roll(g1, 1, 1)
        g2 = pltpu.roll(g1, vertical - 1, 1)
        sum_vert = (f0 + f1) + g1 - 0.5 * (g0 + g2)
        jump = jump + ((f1 - f0) - 0.5 * (g2 - g0))
        at = slice(y * vertical, (y + 1) * vertical)
        mixed[0:8, at] = sum_rad
        mixed[8:16, at] = sum_azi
        mixed[16:24, at] = sum_vert
        total[y] = half_velocity * sum_azi - half_signal * jump_azi - jump
        u1, u2, u3 = u2, u3, u4
        d1, d2 = d2, d3
        s0, s1 = s1, s2
    flux = lax.dot_general(
        weights[...],
        mixed[...],
        (((1,), (0,)), ((), ())),
        precision=lax.Precision.HIGHEST,
        preferred_element_type=F32,
    )
    for y in range(EDGE):
        finish(y, padded[here, y + 2], flux[:, y * vertical : (y + 1) * vertical] + total[y])


def load_padded(field, low_rad, high_rad, low_azi, high_azi, padded, sems):
    middle = pl.ds(2, EDGE)
    copies = [
        (field, padded.at[middle, middle]),
        (low_rad, padded.at[pl.ds(0, 2), middle]),
        (high_rad, padded.at[pl.ds(EDGE + 2, 2), middle]),
        (low_azi, padded.at[middle, pl.ds(0, 2)]),
        (high_azi, padded.at[middle, pl.ds(EDGE + 2, 2)]),
    ]
    copies = [pltpu.make_async_copy(a, b, sems.at[i]) for i, (a, b) in enumerate(copies)]
    for copy in copies:
        copy.start()
    for copy in copies:
        copy.wait()


def first_kernel(
    shear, field, low_rad, high_rad, low_azi, high_azi, mean, weights, ratio, relax,
    state, rad_head, rad_tail, azi_head, azi_tail, sums, padded, mixed, total, sems,
):
    load_padded(field, low_rad, high_rad, low_azi, high_azi, padded, sems)

    def row(x, carry):
        step = ratio[...]
        pull = relax[...]
        average = mean[x]
        column = []

        def finish(y, cell, change):
            value = cell - step * change - pull * (cell - average)
            state[x, y] = value
            if y < 2:
                azi_head[x, y] = value
            if y >= EDGE - 2:
                azi_tail[x, y - (EDGE - 2)] = value
            column.append(value if not column else column.pop() + value)

        stage_row(x, padded, mixed, total, weights, mean, shear, finish)
        sums[x] = column[0]
        return carry

    lax.fori_loop(0, EDGE, row, 0)
    rad_head[...] = state[0:2]
    rad_tail[...] = state[EDGE - 2 : EDGE]


def stage_scratch(vertical):
    return [
        pltpu.VMEM((EDGE + 4, EDGE + 4, CHANNELS, vertical), F32),
        pltpu.VMEM((3 * CHANNELS, EDGE * vertical), F32),
        pltpu.VMEM((EDGE, CHANNELS, vertical), F32),
        pltpu.SemaphoreType.DMA((6,)),
    ]


def first_stage(shear, field, halos, mean, weights, ratio, relax):
    vertical = field.shape[-1]
    return pl.pallas_call(
        first_kernel,
        out_shape=field_shapes(vertical) + [jax.ShapeDtypeStruct((EDGE, CHANNELS, vertical), F32)],
        in_specs=[SMEM] + [ANY] * 5 + [VMEM] * 4,
        out_specs=[VMEM] * 6,
        scratch_shapes=stage_scratch(vertical),
        name="first_stage",
    )(shear, field, *halos, mean, weights, ratio, relax)


def second_kernel(
    shear, start, field, low_rad, high_rad, low_azi, high_azi, mean, weights, ratio, relax,
    final, tendency, padded, mixed, total, sems, change_row, start_field,
):
    begin = pltpu.make_async_copy(start, start_field, sems.at[5])
    begin.start()
    load_padded(field, low_rad, high_rad, low_azi, high_azi, padded, sems)
    begin.wait()
    group = lane_group()
    halves = start.shape[-1] // LANES

    def row(x, carry):
        step = ratio[...]
        pull = relax[...]
        average = mean[x]

        def finish(y, cell, change):
            delta = (cell - start_field[x, y]) - step * change - pull * (cell - average)
            change_row[y] = 0.5 * delta

        stage_row(x, padded, mixed, total, weights, mean, shear, finish)
        base = x * (EDGE * EDGE)
        for half in range(halves):
            lanes = slice(half * LANES, (half + 1) * LANES)
            for upper in range(2):
                at = pl.ds(pl.multiple_of(base + upper * LANES, LANES), LANES)
                deltas = [change_row[upper * 8 + i, :, lanes] for i in range(8)]
                values = [start_field[x, upper * 8 + i, :, lanes] + deltas[i] for i in range(8)]
                for i, tile in enumerate(swap_groups(deltas, group)):
                    tendency[half * 8 + i, :, at] = tile * (1.0 / time_step)
                for i, tile in enumerate(swap_groups(values, group)):
                    final[half * 8 + i, :, at] = tile
        return carry

    lax.fori_loop(0, EDGE, row, 0)


def second_stage(shear, start, field, halos, mean, weights, ratio, relax, out_shape):
    vertical = field.shape[-1]
    return pl.pallas_call(
        second_kernel,
        out_shape=[jax.ShapeDtypeStruct(out_shape, F32)] * 2,
        in_specs=[SMEM] + [ANY] * 6 + [VMEM] * 4,
        out_specs=[VMEM] * 2,
        scratch_shapes=stage_scratch(vertical)
        + [
            pltpu.VMEM((EDGE, CHANNELS, vertical), F32),
            pltpu.VMEM((EDGE, EDGE, CHANNELS, vertical), F32),
        ],
        name="second_stage",
    )(shear, start, field, *halos, mean, weights, ratio, relax)


def sum_azi(values):
    count = lax.axis_size("azi")
    if count & (count - 1):
        return lax.psum(values, "azi")
    step = 1
    while step < count:
        values = values + lax.ppermute(values, "azi", [(i, i ^ step) for i in range(count)])
        step *= 2
    return values


def exchange(rad_head, rad_tail, azi_head, azi_tail):
    rad, azi = lax.axis_size("rad"), lax.axis_size("azi")
    return (
        lax.ppermute(rad_tail, "rad", [(i, i + 1) for i in range(rad - 1)]),
        lax.ppermute(rad_head, "rad", [(i + 1, i) for i in range(rad - 1)]),
        lax.ppermute(azi_tail, "azi", [(i, (i + 1) % azi) for i in range(azi)]),
        lax.ppermute(azi_head, "azi", [((i + 1) % azi, i) for i in range(azi)]),
    )


def on_device(blocks, assignment, levels, coupling, damping):
    azi_count = lax.axis_size("azi")
    rad_count = lax.axis_size("rad")
    azi_index = lax.axis_index("azi")
    rad_index = lax.axis_index("rad")
    block_count = blocks.shape[0]
    vertical = block_count * EDGE
    own = rad_index * azi_count + azi_index
    row_first = rad_index * (azi_count * block_count)
    place = jnp.stack([azi_index, own * block_count, row_first, own]).astype(jnp.int32)

    packed = pack(place, assignment, blocks, azi_count)
    arrived = [
        lax.ppermute(packed[d - 1], "azi", [(i, (i + d) % azi_count) for i in range(azi_count)])
        for d in range(1, azi_count)
    ]
    first_sums, table = column_sums(place, assignment, blocks, azi_count)
    azi_cells = EDGE * azi_count
    first_mean = sum_azi(first_sums) / azi_cells

    factor = jnp.where(levels == 0, 1.0, jnp.where(levels == 1, 2.0, 4.0)).astype(F32) * time_step
    ratio = jnp.broadcast_to(jnp.repeat(factor, EDGE)[None, :], (CHANNELS, vertical))
    relax = jnp.broadcast_to((time_step * damping)[:, None], (CHANNELS, vertical))
    weights = 0.5 * coupling.transpose(1, 0, 2).reshape(CHANNELS, 3 * CHANNELS)
    cells = (rad_index * EDGE + jnp.arange(EDGE)).astype(F32)
    shear = shear_rate * ((cells + 0.5) * (2.0 / (EDGE * rad_count)) - 1.0)

    start, *edges = unpack(table, blocks, arrived, azi_count)
    state, *rest = first_stage(
        shear, start, exchange(*edges), first_mean, weights, ratio, relax
    )
    second_mean = sum_azi(rest[4]) / azi_cells
    final, tendency = second_stage(
        shear, start, state, exchange(*rest[:4]), second_mean, weights, ratio, relax, blocks.shape
    )
    return final, tendency


def solution(mesh):
    in_specs = (P(("rad", "azi"), None, None), P(), P(("rad", "azi")), P(), P())
    out_specs = (P(("rad", "azi"), None, None), P(("rad", "azi"), None, None))
    return jax.shard_map(
        on_device, mesh=mesh, in_specs=in_specs, out_specs=out_specs, check_vma=False
    )
```

```python
import functools

import jax
import jax.numpy as jnp
from jax import lax
from jax.experimental import pallas as pl
from jax.experimental.pallas import tpu as pltpu
from jax.sharding import PartitionSpec as P

EDGE = 16
CHANNELS = 8
CAPACITY = 2
LANES = 128

time_step = 0.02
signal_speed = 2.0
shear_rate = -1.5

ANY = pl.BlockSpec(memory_space=pl.ANY)
SMEM = pl.BlockSpec(memory_space=pltpu.SMEM)
HBM = pl.BlockSpec(memory_space=pltpu.HBM)
VMEM = pl.BlockSpec(memory_space=pltpu.VMEM)
MIB = 1 << 20
COST = pl.CostEstimate(flops=0, bytes_accessed=0, transcendentals=0)
F32 = jnp.float32


def minmod(a, b):
    return jnp.maximum(jnp.minimum(a, b), jnp.minimum(jnp.maximum(a, b), 0.0))


def lane_group():
    return lax.broadcasted_iota(jnp.int32, (CHANNELS, LANES), 1) // EDGE


def swap_groups(rows, group):
    rows = list(rows)
    for bit in (1, 2, 4):
        low = (group & bit) == 0
        shift = EDGE * bit
        for i in range(8):
            if i & bit:
                continue
            a, b = rows[i], rows[i + bit]
            rows[i] = jnp.where(low, a, pltpu.roll(b, shift, 1))
            rows[i + bit] = jnp.where(low, pltpu.roll(a, LANES - shift, 1), b)
    return rows


def own_place():
    azi_count = lax.axis_size("azi")
    azi = lax.axis_index("azi")
    return azi, lax.axis_index("rad") * azi_count + azi


def pack_kernel(azi_count, block_count, assignment, blocks, *refs):
    outs = refs[:azi_count]
    table, sent, fill, sems = refs[azi_count:]
    azi, own = own_place()
    first = own * block_count
    row_first = (own - azi) * block_count
    spots = azi_count * CAPACITY
    for i in range(azi_count):
        fill[i] = 0
    for i in range(spots):
        sent[i] = 0
        table[i] = -1

    def note(j, carry):
        device = lax.div(assignment[first + j], block_count)
        shift = lax.rem(lax.rem(device, azi_count) - azi + azi_count, azi_count)
        k = fill[shift]
        sent[shift * CAPACITY + k] = j
        fill[shift] = k + 1
        return carry

    lax.fori_loop(0, block_count, note, 0)
    copies = []
    for shift in range(azi_count):
        for k in range(CAPACITY):
            spot = shift * CAPACITY + k
            copy = pltpu.make_async_copy(blocks.at[sent[spot]], outs[shift].at[k], sems.at[spot])
            copy.start()
            copies.append(copy)

    def source(s, carry):
        shift = lax.rem(azi - s + azi_count, azi_count)
        start = row_first + s * block_count
        found = jnp.int32(0)
        for j in range(block_count):
            slot = assignment[start + j] - first
            ours = (slot >= 0) & (slot < block_count)
            table[jnp.where(ours, shift * CAPACITY + found, spots)] = slot
            found = found + ours.astype(jnp.int32)
        return carry

    lax.fori_loop(0, azi_count, source, 0)
    for copy in copies:
        copy.wait()


def pack(assignment, blocks, azi_count):
    shape = (CAPACITY,) + blocks.shape[1:]
    spots = azi_count * CAPACITY
    *packed, table = pl.pallas_call(
        functools.partial(pack_kernel, azi_count, blocks.shape[0]),
        out_shape=[pltpu.VMEM(shape, F32)] * azi_count
        + [jax.ShapeDtypeStruct((spots + 1,), jnp.int32)],
        in_specs=[SMEM, HBM],
        out_specs=[VMEM] * azi_count + [SMEM],
        scratch_shapes=[
            pltpu.SMEM((spots,), jnp.int32),
            pltpu.SMEM((azi_count,), jnp.int32),
            pltpu.SemaphoreType.DMA((spots,)),
        ],
        compiler_params=pltpu.CompilerParams(vmem_limit_bytes=4 * MIB),
        name="pack",
    )(assignment, pltpu.with_memory_space_constraint(blocks, pltpu.HBM))
    return packed, table


def coefficients(block_count, levels, damping, coupling, weights, ratio, relax):
    group = lane_group()
    for d in range(3):
        weights[:, d * CHANNELS : (d + 1) * CHANNELS] = 0.5 * coupling[d]
    for half in range(block_count // 8):
        factor = jnp.zeros((CHANNELS, LANES), F32)
        for i in range(8):
            level = levels[half * 8 + i]
            scale = jnp.where(level == 0, 1.0, jnp.where(level == 1, 2.0, 4.0)) * time_step
            factor = jnp.where(group == i, scale, factor)
        ratio[:, half * LANES : (half + 1) * LANES] = factor
    channel = lax.broadcasted_iota(jnp.int32, relax.shape, 0)
    pull = jnp.zeros(relax.shape, F32)
    for c in range(CHANNELS):
        pull = jnp.where(channel == c, time_step * damping[c], pull)
    relax[...] = pull


def unpack_kernel(azi_count, block_count, table, levels, damping, coupling, *refs):
    arrived = refs[:azi_count]
    field, rad_head, rad_tail, azi_head, azi_tail, sums, held, weights, ratio, relax, sems = refs[
        azi_count:
    ]

    def copy_of(shift, k):
        spot = shift * CAPACITY + k
        slot = jnp.maximum(table[spot], 0)
        return pltpu.make_async_copy(arrived[shift].at[k], held.at[slot], sems.at[spot])

    spots = [(shift, k) for shift in range(azi_count) for k in range(CAPACITY)]
    for shift, k in spots:

        @pl.when(table[shift * CAPACITY + k] >= 0)
        def _(shift=shift, k=k):
            copy_of(shift, k).start()

    coefficients(block_count, levels, damping, coupling, weights, ratio, relax)
    for shift, k in spots:

        @pl.when(table[shift * CAPACITY + k] >= 0)
        def _(shift=shift, k=k):
            copy_of(shift, k).wait()

    group = lane_group()

    def row(x, carry):
        base = x * (EDGE * EDGE)
        for half in range(block_count // 8):
            lanes = slice(half * LANES, (half + 1) * LANES)
            running = None
            for upper in range(2):
                at = pl.ds(pl.multiple_of(base + upper * LANES, LANES), LANES)
                tiles = swap_groups([held[half * 8 + i, :, at] for i in range(8)], group)
                for i in range(8):
                    field[x, upper * 8 + i, :, lanes] = tiles[i]
                    running = tiles[i] if running is None else running + tiles[i]
                for i in range(2):
                    if upper == 0:
                        azi_head[x, i, :, lanes] = tiles[i]
                    else:
                        azi_tail[x, i, :, lanes] = tiles[6 + i]
            sums[x, :, lanes] = running
        return carry

    lax.fori_loop(0, EDGE, row, 0)
    rad_head[...] = field[0:2]
    rad_tail[...] = field[EDGE - 2 : EDGE]


def field_shapes(vertical):
    rad = pltpu.VMEM((2, EDGE, CHANNELS, vertical), F32)
    azi = pltpu.VMEM((EDGE, 2, CHANNELS, vertical), F32)
    field = pltpu.VMEM((EDGE, EDGE, CHANNELS, vertical), F32)
    return [field, rad, rad, azi, azi, pltpu.VMEM((EDGE, CHANNELS, vertical), F32)]


def unpack(table, levels, damping, coupling, arrived, block_shape):
    azi_count = len(arrived)
    vertical = block_shape[0] * EDGE
    return pl.pallas_call(
        functools.partial(unpack_kernel, azi_count, block_shape[0]),
        out_shape=field_shapes(vertical)
        + [
            pltpu.VMEM(block_shape, F32),
            pltpu.VMEM((CHANNELS, 3 * CHANNELS), F32),
            pltpu.VMEM((CHANNELS, vertical), F32),
            pltpu.VMEM((CHANNELS, vertical), F32),
        ],
        in_specs=[SMEM, SMEM, SMEM, VMEM] + [ANY] * azi_count,
        out_specs=[VMEM] * 10,
        scratch_shapes=[pltpu.SemaphoreType.DMA((azi_count * CAPACITY,))],
        compiler_params=pltpu.CompilerParams(vmem_limit_bytes=16 * MIB),
        name="unpack",
    )(table, levels, damping, coupling, *arrived)


def shear_of(x):
    cell = (lax.axis_index("rad") * EDGE + x).astype(F32)
    return shear_rate * ((cell + 0.5) * (2.0 / (EDGE * lax.axis_size("rad"))) - 1.0)


def mean_of(sums, x):
    return sums[x] * (1.0 / (EDGE * lax.axis_size("azi")))


def start_radius(get, x, y, carry_slope, carry_plus):
    u = [get(x + i, y) for i in (-2, -1, 0, 1)]
    e = [u[i + 1] - u[i] for i in range(3)]
    before, slope = minmod(e[0], e[1]), minmod(e[1], e[2])
    carry_slope[y] = slope
    carry_plus[y] = e[1] + 0.5 * (slope - before)


def stage_row(get, x, cells, carry_slope, carry_plus, left, step, pull, outs):
    settled, sums_azi, jumps_azi = outs
    low = cells[0]
    u = [get(x, low + i) for i in (-2, -1, 0, 1)]
    vertical = u[0].shape[-1]
    e = [u[i + 1] - u[i] for i in range(3)]
    before, slope = minmod(e[0], e[1]), minmod(e[1], e[2])
    plus = e[1] + 0.5 * (slope - before)
    cell, upper, face = u[2], u[3], e[2]
    for y in cells:
        beyond = get(x, y + 2)
        face_next = beyond - upper
        slope_next = minmod(face, face_next)
        k = 0.5 * (slope_next - slope)
        minus = face - k
        sum_azi = plus + minus
        jump_azi = minus - plus
        plus = face + k
        slope, face = slope_next, face_next
        r1, r2 = get(x + 1, y), get(x + 2, y)
        e1 = r1 - cell
        s1 = minmod(e1, r2 - r1)
        k = 0.5 * (s1 - carry_slope[y])
        minus = e1 - k
        before = carry_plus[y]
        sum_rad = before + minus
        jump = minus - before
        carry_plus[y] = e1 + k
        carry_slope[y] = s1
        f1 = pltpu.roll(cell, vertical - 1, 1) - cell
        g1 = minmod(pltpu.roll(f1, 1, 1), f1)
        k = 0.5 * (pltpu.roll(g1, vertical - 1, 1) - g1)
        minus = f1 - k
        before = pltpu.roll(f1 + k, 1, 1)
        sum_vert = before + minus
        jump = jump + (minus - before)
        stack = []
        for part in (sum_rad, sum_azi, sum_vert):
            high = part.astype(jnp.bfloat16).astype(F32)
            stack += [high, part - high]
        stack = jnp.concatenate(stack, axis=0).astype(jnp.bfloat16)
        pair = lax.dot_general(left, stack, (((1,), (0,)), ((), ())), preferred_element_type=F32)
        flux = (pair[:CHANNELS] + pair[CHANNELS:]) - jump
        settled[x, y] = cell - step * flux - pull * cell
        sums_azi[x, y] = step * sum_azi
        jumps_azi[x, y] = step * jump_azi
        cell, upper = upper, beyond


def split_weights(weights):
    w = weights[...]
    high = w.astype(jnp.bfloat16).astype(F32)
    both = jnp.concatenate([high, w - high], axis=0)
    columns = [both[:, CHANNELS * (i // 2) : CHANNELS * (i // 2 + 1)] for i in range(6)]
    return jnp.concatenate(columns, axis=1).astype(jnp.bfloat16)


def sweep(get, rows, runs, carry_slope, carry_plus, left, ratio, relax, outs):
    for cells in runs:
        for y in cells:
            start_radius(get, rows[0], y, carry_slope, carry_plus)

    def row(x, carry):
        for cells in runs:
            stage_row(
                get, x, cells, carry_slope, carry_plus, left, ratio[...], relax[...], outs
            )
        return carry

    lax.fori_loop(rows[0], rows[1], row, 0)


INNER = range(2, EDGE - 2)
HEAD, TAIL = range(0, 2), range(EDGE - 2, EDGE)


def inner_kernel(field, weights, ratio, relax, *refs):
    outs, carries = refs[:3], refs[3:]

    def get(x, y):
        return field[x, y]

    sweep(get, (2, EDGE - 2), (INNER,), *carries, split_weights(weights), ratio, relax, outs)


def inner_stage(field, weights, ratio, relax):
    vertical = field.shape[-1]
    return pl.pallas_call(
        inner_kernel,
        out_shape=[pltpu.VMEM(field.shape, F32)] * 3,
        in_specs=[VMEM] * 4,
        out_specs=[VMEM] * 3,
        scratch_shapes=[pltpu.VMEM((EDGE, CHANNELS, vertical), F32)] * 2,
        compiler_params=pltpu.CompilerParams(vmem_limit_bytes=16 * MIB),
        cost_estimate=COST,
        name="inner_stage",
    )(field, weights, ratio, relax)


def outer_kernel(
    field, low_rad, high_rad, low_azi, high_azi, weights, ratio, relax, one, two, three, *refs
):
    del one, two, three
    outs = refs[:3]
    padded, carry_slope, carry_plus, sems = refs[3:]
    load_padded(field, low_rad, high_rad, low_azi, high_azi, padded, sems)

    def get(x, y):
        return padded[x + 2, y + 2]

    rest = (carry_slope, carry_plus, split_weights(weights), ratio, relax, outs)
    sweep(get, (0, 2), (range(EDGE),), *rest)
    sweep(get, (2, EDGE - 2), (HEAD, TAIL), *rest)
    sweep(get, (EDGE - 2, EDGE), (range(EDGE),), *rest)


def outer_stage(field, halos, weights, ratio, relax, parts):
    vertical = field.shape[-1]
    return pl.pallas_call(
        outer_kernel,
        out_shape=[pltpu.VMEM(field.shape, F32)] * 3,
        in_specs=[ANY] * 5 + [VMEM] * 6,
        out_specs=[VMEM] * 3,
        scratch_shapes=[
            pltpu.VMEM((EDGE + 4, EDGE + 4, CHANNELS, vertical), F32),
            pltpu.VMEM((EDGE, CHANNELS, vertical), F32),
            pltpu.VMEM((EDGE, CHANNELS, vertical), F32),
            pltpu.SemaphoreType.DMA((5,)),
        ],
        input_output_aliases={8: 0, 9: 1, 10: 2},
        compiler_params=pltpu.CompilerParams(vmem_limit_bytes=16 * MIB),
        cost_estimate=COST,
        name="outer_stage",
    )(field, *halos, weights, ratio, relax, *parts)


def speeds(average, x):
    velocity = jnp.broadcast_to(average[2:3, :], average.shape) + shear_of(x)
    return 0.5 * velocity, 0.5 * jnp.abs(velocity) + 0.5 * signal_speed


def split_weights(weights):
    w = weights[...]
    high = w.astype(jnp.bfloat16).astype(F32)
    both = jnp.concatenate([high, w - high], axis=0)
    columns = [both[:, CHANNELS * (i // 2) : CHANNELS * (i // 2 + 1)] for i in range(6)]
    return jnp.concatenate(columns, axis=1).astype(jnp.bfloat16)


def load_padded(field, low_rad, high_rad, low_azi, high_azi, padded, sems):
    middle = pl.ds(2, EDGE)
    copies = [
        (field, padded.at[middle, middle]),
        (low_rad, padded.at[pl.ds(0, 2), middle]),
        (high_rad, padded.at[pl.ds(EDGE + 2, 2), middle]),
        (low_azi, padded.at[middle, pl.ds(0, 2)]),
        (high_azi, padded.at[middle, pl.ds(EDGE + 2, 2)]),
    ]
    copies = [pltpu.make_async_copy(a, b, sems.at[i]) for i, (a, b) in enumerate(copies)]
    for copy in copies:
        copy.start()
    for copy in copies:
        copy.wait()


def join_kernel(
    settled, sums_azi, jumps_azi, column, relax,
    state, rad_head, rad_tail, azi_head, azi_tail, sums,
):
    def row(x, carry):
        average = mean_of(column, x)
        half_velocity, half_signal = speeds(average, x)
        pulled = relax[...] * average
        running = None
        for y in range(EDGE):
            value = (
                (settled[x, y] + pulled)
                - half_velocity * sums_azi[x, y]
                + half_signal * jumps_azi[x, y]
            )
            state[x, y] = value
            if y < 2:
                azi_head[x, y] = value
            if y >= EDGE - 2:
                azi_tail[x, y - (EDGE - 2)] = value
            running = value if running is None else running + value
        sums[x] = running
        return carry

    lax.fori_loop(0, EDGE, row, 0)
    rad_head[...] = state[0:2]
    rad_tail[...] = state[EDGE - 2 : EDGE]


def join_stage(parts, column, relax):
    vertical = parts[0].shape[-1]
    return pl.pallas_call(
        join_kernel,
        out_shape=field_shapes(vertical),
        in_specs=[VMEM] * 5,
        out_specs=[VMEM] * 6,
        compiler_params=pltpu.CompilerParams(vmem_limit_bytes=8 * MIB),
        name="join_stage",
    )(*parts, column, relax)


def final_kernel(
    held, settled, sums_azi, jumps_azi, column, relax,
    final, tendency, final_rows, tendency_rows, out_sems,
):
    group = lane_group()
    halves = held.shape[0] // 8

    def out_copies(x):
        at = pl.ds(pl.multiple_of(x * (EDGE * EDGE), LANES), EDGE * EDGE)
        return [
            pltpu.make_async_copy(a.at[:, :, at], b.at[:, :, at], out_sems.at[i, x])
            for i, (a, b) in enumerate(((final_rows, final), (tendency_rows, tendency)))
        ]

    def row(x, carry):
        average = mean_of(column, x)
        half_velocity, half_signal = speeds(average, x)
        pulled = relax[...] * average
        base = x * (EDGE * EDGE)
        for half in range(halves):
            lanes = slice(half * LANES, (half + 1) * LANES)
            for upper in range(2):
                at = pl.ds(pl.multiple_of(base + upper * LANES, LANES), LANES)
                results = []
                for i in range(8):
                    y = upper * 8 + i
                    results.append(
                        (settled[x, y, :, lanes] + pulled[:, lanes])
                        - half_velocity[:, lanes] * sums_azi[x, y, :, lanes]
                        + half_signal[:, lanes] * jumps_azi[x, y, :, lanes]
                    )
                for i, tile in enumerate(swap_groups(results, group)):
                    start = held[half * 8 + i, :, at]
                    change = 0.5 * (tile - start)
                    final_rows[half * 8 + i, :, at] = start + change
                    tendency_rows[half * 8 + i, :, at] = change * (1.0 / time_step)
        for copy in out_copies(x):
            copy.start()
        return carry

    lax.fori_loop(0, EDGE, row, 0)

    def finish_row(x, carry):
        for copy in out_copies(x):
            copy.wait()
        return carry

    lax.fori_loop(0, EDGE, finish_row, 0)


def final_stage(held, parts, column, relax):
    return pl.pallas_call(
        final_kernel,
        out_shape=[jax.ShapeDtypeStruct(held.shape, F32)] * 2,
        in_specs=[VMEM] * 6,
        out_specs=[HBM] * 2,
        scratch_shapes=[
            pltpu.VMEM(held.shape, F32),
            pltpu.VMEM(held.shape, F32),
            pltpu.SemaphoreType.DMA((2, EDGE)),
        ],
        compiler_params=pltpu.CompilerParams(vmem_limit_bytes=8 * MIB),
        name="final_stage",
    )(held, *parts, column, relax)


def sum_azi(values, beside):
    count = lax.axis_size("azi")
    if count & (count - 1):
        return lax.psum(values, "azi"), beside
    step = 1
    while step < count:
        other = lax.ppermute(values, "azi", [(i, i ^ step) for i in range(count)])
        if step == 2:
            other, beside = lax.optimization_barrier((other, beside))
        values = values + other
        step *= 2
    return values, beside


def exchange(rad_head, rad_tail, azi_head, azi_tail):
    rad, azi = lax.axis_size("rad"), lax.axis_size("azi")
    return (
        lax.ppermute(rad_tail, "rad", [(i, i + 1) for i in range(rad - 1)]),
        lax.ppermute(rad_head, "rad", [(i + 1, i) for i in range(rad - 1)]),
        lax.ppermute(azi_tail, "azi", [(i, (i + 1) % azi) for i in range(azi)]),
        lax.ppermute(azi_head, "azi", [((i + 1) % azi, i) for i in range(azi)]),
    )


def on_device(blocks, assignment, levels, coupling, damping):
    azi_count = lax.axis_size("azi")
    packed, table = pack(assignment, blocks, azi_count)
    arrived = [packed[0]] + [
        lax.ppermute(packed[d], "azi", [(i, (i + d) % azi_count) for i in range(azi_count)])
        for d in range(1, azi_count)
    ]
    start, *edges, sums, held, weights, ratio, relax = unpack(
        table, levels, damping, coupling, arrived, blocks.shape
    )

    def section(field, edges, sums):
        halos = exchange(*edges)
        parts = inner_stage(field, weights, ratio, relax)
        column, parts = sum_azi(sums, parts)
        return outer_stage(field, halos, weights, ratio, relax, parts), column

    parts, column = section(start, edges, sums)
    state, *edges, sums = join_stage(parts, column, relax)
    parts, column = section(state, edges, sums)
    return final_stage(held, parts, column, relax)


def solution(mesh):
    in_specs = (P(("rad", "azi"), None, None), P(), P(("rad", "azi")), P(), P())
    out_specs = (P(("rad", "azi"), None, None), P(("rad", "azi"), None, None))
    return jax.shard_map(
        on_device, mesh=mesh, in_specs=in_specs, out_specs=out_specs, check_vma=False
    )
```

```python
import functools

import jax
import jax.numpy as jnp
from jax import lax
from jax.experimental import pallas as pl
from jax.experimental.pallas import tpu as pltpu
from jax.sharding import PartitionSpec as P

EDGE = 16
CHANNELS = 8
CAPACITY = 2
LANES = 128

time_step = 0.02
signal_speed = 2.0
shear_rate = -1.5

ANY = pl.BlockSpec(memory_space=pl.ANY)
SMEM = pl.BlockSpec(memory_space=pltpu.SMEM)
HBM = pl.BlockSpec(memory_space=pltpu.HBM)
VMEM = pl.BlockSpec(memory_space=pltpu.VMEM)
MIB = 1 << 20
COST = pl.CostEstimate(flops=0, bytes_accessed=0, transcendentals=0)
F32 = jnp.float32


def minmod(a, b):
    return jnp.maximum(jnp.minimum(a, b), jnp.minimum(jnp.maximum(a, b), 0.0))


def lane_group():
    return lax.broadcasted_iota(jnp.int32, (CHANNELS, LANES), 1) // EDGE


def swap_groups(rows, group):
    rows = list(rows)
    for bit in (1, 2, 4):
        low = (group & bit) == 0
        shift = EDGE * bit
        for i in range(8):
            if i & bit:
                continue
            a, b = rows[i], rows[i + bit]
            rows[i] = jnp.where(low, a, pltpu.roll(b, shift, 1))
            rows[i + bit] = jnp.where(low, pltpu.roll(a, LANES - shift, 1), b)
    return rows


def own_place():
    azi_count = lax.axis_size("azi")
    azi = lax.axis_index("azi")
    return azi, lax.axis_index("rad") * azi_count + azi


def pack_kernel(azi_count, block_count, assignment, blocks, *refs):
    outs = refs[:azi_count]
    table, sent, fill, sems = refs[azi_count:]
    azi, own = own_place()
    first = own * block_count
    row_first = (own - azi) * block_count
    spots = azi_count * CAPACITY
    for i in range(azi_count):
        fill[i] = 0
    for i in range(spots):
        sent[i] = 0
        table[i] = -1

    def note(j, carry):
        device = lax.div(assignment[first + j], block_count)
        shift = lax.rem(lax.rem(device, azi_count) - azi + azi_count, azi_count)
        k = fill[shift]
        sent[shift * CAPACITY + k] = j
        fill[shift] = k + 1
        return carry

    lax.fori_loop(0, block_count, note, 0)
    copies = []
    for shift in range(azi_count):
        for k in range(CAPACITY):
            spot = shift * CAPACITY + k
            copy = pltpu.make_async_copy(blocks.at[sent[spot]], outs[shift].at[k], sems.at[spot])
            copy.start()
            copies.append(copy)

    def source(s, carry):
        shift = lax.rem(azi - s + azi_count, azi_count)
        start = row_first + s * block_count
        found = jnp.int32(0)
        for j in range(block_count):
            slot = assignment[start + j] - first
            ours = (slot >= 0) & (slot < block_count)
            table[jnp.where(ours, shift * CAPACITY + found, spots)] = slot
            found = found + ours.astype(jnp.int32)
        return carry

    lax.fori_loop(0, azi_count, source, 0)
    for copy in copies:
        copy.wait()


def pack(assignment, blocks, azi_count):
    shape = (CAPACITY,) + blocks.shape[1:]
    spots = azi_count * CAPACITY
    *packed, table = pl.pallas_call(
        functools.partial(pack_kernel, azi_count, blocks.shape[0]),
        out_shape=[pltpu.VMEM(shape, F32)] * azi_count
        + [jax.ShapeDtypeStruct((spots + 1,), jnp.int32)],
        in_specs=[SMEM, HBM],
        out_specs=[VMEM] * azi_count + [SMEM],
        scratch_shapes=[
            pltpu.SMEM((spots,), jnp.int32),
            pltpu.SMEM((azi_count,), jnp.int32),
            pltpu.SemaphoreType.DMA((spots,)),
        ],
        compiler_params=pltpu.CompilerParams(vmem_limit_bytes=4 * MIB),
        name="pack",
    )(assignment, pltpu.with_memory_space_constraint(blocks, pltpu.HBM))
    return packed, table


def coefficients(block_count, levels, damping, coupling, weights, ratio, relax):
    group = lane_group()
    for d in range(3):
        weights[:, d * CHANNELS : (d + 1) * CHANNELS] = 0.5 * coupling[d]
    for half in range(block_count // 8):
        factor = jnp.zeros((CHANNELS, LANES), F32)
        for i in range(8):
            level = levels[half * 8 + i]
            scale = jnp.where(level == 0, 1.0, jnp.where(level == 1, 2.0, 4.0)) * time_step
            factor = jnp.where(group == i, scale, factor)
        ratio[:, half * LANES : (half + 1) * LANES] = factor
    channel = lax.broadcasted_iota(jnp.int32, relax.shape, 0)
    pull = jnp.zeros(relax.shape, F32)
    for c in range(CHANNELS):
        pull = jnp.where(channel == c, time_step * damping[c], pull)
    relax[...] = pull


def order_of(azi_count):
    return [0] + sorted(range(1, azi_count), key=lambda d: abs(2 * d - azi_count))


def unpack_kernel(azi_count, block_count, table, levels, damping, coupling, *refs):
    arrived = {d: refs[i] for i, d in enumerate(order_of(azi_count))}
    field, rad_head, rad_tail, azi_head, azi_tail, sums, held, weights, ratio, relax, sems = refs[
        azi_count:
    ]

    def copy_of(shift, k):
        spot = shift * CAPACITY + k
        slot = jnp.maximum(table[spot], 0)
        return pltpu.make_async_copy(arrived[shift].at[k], held.at[slot], sems.at[spot])

    spots = [(shift, k) for shift in range(azi_count) for k in range(CAPACITY)]
    for shift, k in spots:

        @pl.when(table[shift * CAPACITY + k] >= 0)
        def _(shift=shift, k=k):
            copy_of(shift, k).start()

    coefficients(block_count, levels, damping, coupling, weights, ratio, relax)
    for shift, k in spots:

        @pl.when(table[shift * CAPACITY + k] >= 0)
        def _(shift=shift, k=k):
            copy_of(shift, k).wait()

    group = lane_group()

    def row(x, carry):
        base = x * (EDGE * EDGE)
        for half in range(block_count // 8):
            lanes = slice(half * LANES, (half + 1) * LANES)
            running = None
            for upper in range(2):
                at = pl.ds(pl.multiple_of(base + upper * LANES, LANES), LANES)
                tiles = swap_groups([held[half * 8 + i, :, at] for i in range(8)], group)
                for i in range(8):
                    field[x, upper * 8 + i, :, lanes] = tiles[i]
                    running = tiles[i] if running is None else running + tiles[i]
                for i in range(2):
                    if upper == 0:
                        azi_head[x, i, :, lanes] = tiles[i]
                    else:
                        azi_tail[x, i, :, lanes] = tiles[6 + i]
            sums[x, :, lanes] = running
        return carry

    lax.fori_loop(0, EDGE, row, 0, unroll=2)
    rad_head[...] = field[0:2]
    rad_tail[...] = field[EDGE - 2 : EDGE]


def field_shapes(vertical):
    rad = pltpu.VMEM((2, EDGE, CHANNELS, vertical), F32)
    azi = pltpu.VMEM((EDGE, 2, CHANNELS, vertical), F32)
    field = pltpu.VMEM((EDGE, EDGE, CHANNELS, vertical), F32)
    return [field, rad, rad, azi, azi, pltpu.VMEM((EDGE, CHANNELS, vertical), F32)]


def unpack(table, levels, damping, coupling, arrived, block_shape):
    azi_count = len(arrived)
    vertical = block_shape[0] * EDGE
    return pl.pallas_call(
        functools.partial(unpack_kernel, azi_count, block_shape[0]),
        out_shape=field_shapes(vertical)
        + [
            pltpu.VMEM(block_shape, F32),
            pltpu.VMEM((CHANNELS, 3 * CHANNELS), F32),
            pltpu.VMEM((CHANNELS, vertical), F32),
            pltpu.VMEM((CHANNELS, vertical), F32),
        ],
        in_specs=[SMEM, SMEM, SMEM, VMEM] + [ANY] * azi_count,
        out_specs=[VMEM] * 10,
        scratch_shapes=[pltpu.SemaphoreType.DMA((azi_count * CAPACITY,))],
        compiler_params=pltpu.CompilerParams(vmem_limit_bytes=16 * MIB),
        name="unpack",
    )(table, levels, damping, coupling, *(arrived[d] for d in order_of(azi_count)))


def shear_of(x):
    cell = (lax.axis_index("rad") * EDGE + x).astype(F32)
    return shear_rate * ((cell + 0.5) * (2.0 / (EDGE * lax.axis_size("rad"))) - 1.0)


def mean_of(sums, x):
    return sums[x] * (1.0 / (EDGE * lax.axis_size("azi")))


def start_radius(get, x, y, carry_slope, carry_plus):
    u = [get(x + i, y) for i in (-2, -1, 0, 1)]
    e = [u[i + 1] - u[i] for i in range(3)]
    before, slope = minmod(e[0], e[1]), minmod(e[1], e[2])
    carry_slope[y] = slope
    carry_plus[y] = e[1] + 0.5 * (slope - before)


def stage_row(get, x, cells, carry_slope, carry_plus, left, step, pull, outs):
    settled, sums_azi, jumps_azi = outs
    low = cells[0]
    u = [get(x, low + i) for i in (-2, -1, 0, 1)]
    vertical = u[0].shape[-1]
    e = [u[i + 1] - u[i] for i in range(3)]
    before, slope = minmod(e[0], e[1]), minmod(e[1], e[2])
    plus = e[1] + 0.5 * (slope - before)
    cell, upper, face = u[2], u[3], e[2]
    for y in cells:
        beyond = get(x, y + 2)
        face_next = beyond - upper
        slope_next = minmod(face, face_next)
        k = 0.5 * (slope_next - slope)
        minus = face - k
        sum_azi = plus + minus
        jump_azi = minus - plus
        plus = face + k
        slope, face = slope_next, face_next
        r1, r2 = get(x + 1, y), get(x + 2, y)
        e1 = r1 - cell
        s1 = minmod(e1, r2 - r1)
        k = 0.5 * (s1 - carry_slope[y])
        minus = e1 - k
        before = carry_plus[y]
        sum_rad = before + minus
        jump = minus - before
        carry_plus[y] = e1 + k
        carry_slope[y] = s1
        f1 = pltpu.roll(cell, vertical - 1, 1) - cell
        g1 = minmod(pltpu.roll(f1, 1, 1), f1)
        k = 0.5 * (pltpu.roll(g1, vertical - 1, 1) - g1)
        minus = f1 - k
        before = pltpu.roll(f1 + k, 1, 1)
        sum_vert = before + minus
        jump = jump + (minus - before)
        stack = []
        for part in (sum_rad, sum_azi, sum_vert):
            high = part.astype(jnp.bfloat16).astype(F32)
            stack += [high, part - high]
        stack = jnp.concatenate(stack, axis=0).astype(jnp.bfloat16)
        pair = lax.dot_general(left, stack, (((1,), (0,)), ((), ())), preferred_element_type=F32)
        flux = (pair[:CHANNELS] + pair[CHANNELS:]) - jump
        settled[x, y] = cell - step * flux - pull * cell
        sums_azi[x, y] = step * sum_azi
        jumps_azi[x, y] = step * jump_azi
        cell, upper = upper, beyond


def split_weights(weights):
    w = weights[...]
    high = w.astype(jnp.bfloat16).astype(F32)
    both = jnp.concatenate([high, w - high], axis=0)
    columns = [both[:, CHANNELS * (i // 2) : CHANNELS * (i // 2 + 1)] for i in range(6)]
    return jnp.concatenate(columns, axis=1).astype(jnp.bfloat16)


def sweep(get, rows, runs, carry_slope, carry_plus, left, ratio, relax, outs, unroll=1):
    for cells in runs:
        for y in cells:
            start_radius(get, rows[0], y, carry_slope, carry_plus)

    def row(x, carry):
        for cells in runs:
            stage_row(
                get, x, cells, carry_slope, carry_plus, left, ratio[...], relax[...], outs
            )
        return carry

    lax.fori_loop(rows[0], rows[1], row, 0, unroll=unroll)


INNER = range(2, EDGE - 2)
HEAD, TAIL = range(0, 2), range(EDGE - 2, EDGE)


def inner_kernel(field, weights, ratio, relax, *refs):
    outs, carries = refs[:3], refs[3:]

    def get(x, y):
        return field[x, y]

    sweep(get, (2, EDGE - 2), (INNER,), *carries, split_weights(weights), ratio, relax, outs, unroll=4)


def inner_stage(field, weights, ratio, relax):
    vertical = field.shape[-1]
    return pl.pallas_call(
        inner_kernel,
        out_shape=[pltpu.VMEM(field.shape, F32)] * 3,
        in_specs=[VMEM] * 4,
        out_specs=[VMEM] * 3,
        scratch_shapes=[pltpu.VMEM((EDGE, CHANNELS, vertical), F32)] * 2,
        compiler_params=pltpu.CompilerParams(vmem_limit_bytes=16 * MIB),
        cost_estimate=COST,
        name="inner_stage",
    )(field, weights, ratio, relax)


def outer_kernel(
    field, low_azi, high_azi, low_rad, high_rad, weights, ratio, relax, one, two, three, *refs
):
    del one, two, three
    outs = refs[:3]
    padded, carry_slope, carry_plus, sems = refs[3:]
    load_padded(field, low_rad, high_rad, low_azi, high_azi, padded, sems)

    def get(x, y):
        return padded[x + 2, y + 2]

    rest = (carry_slope, carry_plus, split_weights(weights), ratio, relax, outs)
    sweep(get, (0, 2), (range(EDGE),), *rest)
    sweep(get, (2, EDGE - 2), (HEAD, TAIL), *rest, unroll=12)
    sweep(get, (EDGE - 2, EDGE), (range(EDGE),), *rest)


def outer_stage(field, halos, weights, ratio, relax, parts):
    vertical = field.shape[-1]
    return pl.pallas_call(
        outer_kernel,
        out_shape=[pltpu.VMEM(field.shape, F32)] * 3,
        in_specs=[ANY] * 5 + [VMEM] * 6,
        out_specs=[VMEM] * 3,
        scratch_shapes=[
            pltpu.VMEM((EDGE + 4, EDGE + 4, CHANNELS, vertical), F32),
            pltpu.VMEM((EDGE, CHANNELS, vertical), F32),
            pltpu.VMEM((EDGE, CHANNELS, vertical), F32),
            pltpu.SemaphoreType.DMA((5,)),
        ],
        input_output_aliases={8: 0, 9: 1, 10: 2},
        compiler_params=pltpu.CompilerParams(vmem_limit_bytes=16 * MIB),
        cost_estimate=COST,
        name="outer_stage",
    )(field, *halos, weights, ratio, relax, *parts)


def speeds(average, x):
    velocity = jnp.broadcast_to(average[2:3, :], average.shape) + shear_of(x)
    return 0.5 * velocity, 0.5 * jnp.abs(velocity) + 0.5 * signal_speed


def split_weights(weights):
    w = weights[...]
    high = w.astype(jnp.bfloat16).astype(F32)
    both = jnp.concatenate([high, w - high], axis=0)
    columns = [both[:, CHANNELS * (i // 2) : CHANNELS * (i // 2 + 1)] for i in range(6)]
    return jnp.concatenate(columns, axis=1).astype(jnp.bfloat16)


def load_padded(field, low_rad, high_rad, low_azi, high_azi, padded, sems):
    middle = pl.ds(2, EDGE)
    copies = [
        (field, padded.at[middle, middle]),
        (low_rad, padded.at[pl.ds(0, 2), middle]),
        (high_rad, padded.at[pl.ds(EDGE + 2, 2), middle]),
        (low_azi, padded.at[middle, pl.ds(0, 2)]),
        (high_azi, padded.at[middle, pl.ds(EDGE + 2, 2)]),
    ]
    copies = [pltpu.make_async_copy(a, b, sems.at[i]) for i, (a, b) in enumerate(copies)]
    for copy in copies:
        copy.start()
    for copy in copies:
        copy.wait()


def join_kernel(
    settled, sums_azi, jumps_azi, column, relax,
    state, rad_head, rad_tail, azi_head, azi_tail, sums,
):
    def row(x, carry):
        average = mean_of(column, x)
        half_velocity, half_signal = speeds(average, x)
        pulled = relax[...] * average
        running = None
        for y in range(EDGE):
            value = (
                (settled[x, y] + pulled)
                - half_velocity * sums_azi[x, y]
                + half_signal * jumps_azi[x, y]
            )
            state[x, y] = value
            if y < 2:
                azi_head[x, y] = value
            if y >= EDGE - 2:
                azi_tail[x, y - (EDGE - 2)] = value
            running = value if running is None else running + value
        sums[x] = running
        return carry

    lax.fori_loop(0, EDGE, row, 0)
    rad_head[...] = state[0:2]
    rad_tail[...] = state[EDGE - 2 : EDGE]


def join_stage(parts, column, relax):
    vertical = parts[0].shape[-1]
    return pl.pallas_call(
        join_kernel,
        out_shape=field_shapes(vertical),
        in_specs=[VMEM] * 5,
        out_specs=[VMEM] * 6,
        compiler_params=pltpu.CompilerParams(vmem_limit_bytes=8 * MIB),
        name="join_stage",
    )(*parts, column, relax)


def final_kernel(
    held, settled, sums_azi, jumps_azi, column, relax,
    final, tendency, final_rows, tendency_rows, out_sems,
):
    group = lane_group()
    halves = held.shape[0] // 8

    def out_copies(x):
        at = pl.ds(pl.multiple_of(x * (EDGE * EDGE), LANES), EDGE * EDGE)
        return [
            pltpu.make_async_copy(a.at[:, :, at], b.at[:, :, at], out_sems.at[i, x])
            for i, (a, b) in enumerate(((final_rows, final), (tendency_rows, tendency)))
        ]

    def row(x, carry):
        average = mean_of(column, x)
        half_velocity, half_signal = speeds(average, x)
        pulled = relax[...] * average
        base = x * (EDGE * EDGE)
        for half in range(halves):
            lanes = slice(half * LANES, (half + 1) * LANES)
            for upper in range(2):
                at = pl.ds(pl.multiple_of(base + upper * LANES, LANES), LANES)
                results = []
                for i in range(8):
                    y = upper * 8 + i
                    results.append(
                        (settled[x, y, :, lanes] + pulled[:, lanes])
                        - half_velocity[:, lanes] * sums_azi[x, y, :, lanes]
                        + half_signal[:, lanes] * jumps_azi[x, y, :, lanes]
                    )
                for i, tile in enumerate(swap_groups(results, group)):
                    start = held[half * 8 + i, :, at]
                    change = 0.5 * (tile - start)
                    final_rows[half * 8 + i, :, at] = start + change
                    tendency_rows[half * 8 + i, :, at] = change * (1.0 / time_step)
        for copy in out_copies(x):
            copy.start()
        return carry

    lax.fori_loop(0, EDGE, row, 0, unroll=2)

    def finish_row(x, carry):
        for copy in out_copies(x):
            copy.wait()
        return carry

    lax.fori_loop(0, EDGE, finish_row, 0)


def final_stage(held, parts, column, relax):
    return pl.pallas_call(
        final_kernel,
        out_shape=[jax.ShapeDtypeStruct(held.shape, F32)] * 2,
        in_specs=[VMEM] * 6,
        out_specs=[HBM] * 2,
        scratch_shapes=[
            pltpu.VMEM(held.shape, F32),
            pltpu.VMEM(held.shape, F32),
            pltpu.SemaphoreType.DMA((2, EDGE)),
        ],
        compiler_params=pltpu.CompilerParams(vmem_limit_bytes=8 * MIB),
        name="final_stage",
    )(held, *parts, column, relax)


def sum_azi(values, beside):
    count = lax.axis_size("azi")
    if count & (count - 1):
        return lax.psum(values, "azi"), beside
    step = 1
    while step < count:
        other = lax.ppermute(values, "azi", [(i, i ^ step) for i in range(count)])
        if step == 2:
            other, beside = lax.optimization_barrier((other, beside))
        values = values + other
        step *= 2
    return values, beside


def exchange(rad_head, rad_tail, azi_head, azi_tail):
    rad, azi = lax.axis_size("rad"), lax.axis_size("azi")
    return (
        lax.ppermute(azi_tail, "azi", [(i, (i + 1) % azi) for i in range(azi)]),
        lax.ppermute(azi_head, "azi", [((i + 1) % azi, i) for i in range(azi)]),
        lax.ppermute(rad_tail, "rad", [(i, i + 1) for i in range(rad - 1)]),
        lax.ppermute(rad_head, "rad", [(i + 1, i) for i in range(rad - 1)]),
    )


def on_device(blocks, assignment, levels, coupling, damping):
    azi_count = lax.axis_size("azi")
    packed, table = pack(assignment, blocks, azi_count)
    arrived = [packed[0]] + [
        lax.ppermute(packed[d], "azi", [(i, (i + d) % azi_count) for i in range(azi_count)])
        for d in range(1, azi_count)
    ]
    start, *edges, sums, held, weights, ratio, relax = unpack(
        table, levels, damping, coupling, arrived, blocks.shape
    )

    def section(field, edges, sums):
        halos = exchange(*edges)
        parts = inner_stage(field, weights, ratio, relax)
        column, parts = sum_azi(sums, parts)
        return outer_stage(field, halos, weights, ratio, relax, parts), column

    parts, column = section(start, edges, sums)
    state, *edges, sums = join_stage(parts, column, relax)
    parts, column = section(state, edges, sums)
    return final_stage(held, parts, column, relax)


def solution(mesh):
    in_specs = (P(("rad", "azi"), None, None), P(), P(("rad", "azi")), P(), P())
    out_specs = (P(("rad", "azi"), None, None), P(("rad", "azi"), None, None))
    return jax.shard_map(
        on_device, mesh=mesh, in_specs=in_specs, out_specs=out_specs, check_vma=False
    )
```

```python
import functools

import jax
import jax.numpy as jnp
from jax import lax
from jax.experimental import pallas as pl
from jax.experimental.pallas import tpu as pltpu
from jax.sharding import PartitionSpec as P

EDGE = 16
CHANNELS = 8
CAPACITY = 2
LANES = 128

time_step = 0.02
signal_speed = 2.0
shear_rate = -1.5

ANY = pl.BlockSpec(memory_space=pl.ANY)
SMEM = pl.BlockSpec(memory_space=pltpu.SMEM)
HBM = pl.BlockSpec(memory_space=pltpu.HBM)
VMEM = pl.BlockSpec(memory_space=pltpu.VMEM)
MIB = 1 << 20
COST = pl.CostEstimate(flops=0, bytes_accessed=0, transcendentals=0)
F32 = jnp.float32


def minmod(a, b):
    return jnp.maximum(jnp.minimum(a, b), jnp.minimum(jnp.maximum(a, b), 0.0))


def lane_group():
    return lax.broadcasted_iota(jnp.int32, (CHANNELS, LANES), 1) // EDGE


def swap_groups(rows, group):
    rows = list(rows)
    for bit in (1, 2, 4):
        low = (group & bit) == 0
        shift = EDGE * bit
        for i in range(8):
            if i & bit:
                continue
            a, b = rows[i], rows[i + bit]
            rows[i] = jnp.where(low, a, pltpu.roll(b, shift, 1))
            rows[i + bit] = jnp.where(low, pltpu.roll(a, LANES - shift, 1), b)
    return rows


def own_place():
    azi_count = lax.axis_size("azi")
    azi = lax.axis_index("azi")
    return azi, lax.axis_index("rad") * azi_count + azi


def pack_kernel(azi_count, block_count, assignment, blocks, *refs):
    outs = refs[:azi_count]
    table, sent, fill, sems = refs[azi_count:]
    azi, own = own_place()
    first = own * block_count
    row_first = (own - azi) * block_count
    spots = azi_count * CAPACITY
    for i in range(azi_count):
        fill[i] = 0
    for i in range(spots):
        sent[i] = 0
        table[i] = -1

    def note(j, carry):
        device = lax.div(assignment[first + j], block_count)
        shift = lax.rem(lax.rem(device, azi_count) - azi + azi_count, azi_count)
        k = fill[shift]
        sent[shift * CAPACITY + k] = j
        fill[shift] = k + 1
        return carry

    lax.fori_loop(0, block_count, note, 0, unroll=True)
    copies = []
    for shift in range(azi_count):
        for k in range(CAPACITY):
            spot = shift * CAPACITY + k
            copy = pltpu.make_async_copy(blocks.at[sent[spot]], outs[shift].at[k], sems.at[spot])
            copy.start()
            copies.append(copy)

    def source(s, carry):
        shift = lax.rem(azi - s + azi_count, azi_count)
        start = row_first + s * block_count
        found = jnp.int32(0)
        for j in range(block_count):
            slot = assignment[start + j] - first
            ours = (slot >= 0) & (slot < block_count)
            table[jnp.where(ours, shift * CAPACITY + found, spots)] = slot
            found = found + ours.astype(jnp.int32)
        return carry

    lax.fori_loop(0, azi_count, source, 0)
    for copy in copies:
        copy.wait()


def pack(assignment, blocks, azi_count):
    shape = (CAPACITY,) + blocks.shape[1:]
    spots = azi_count * CAPACITY
    *packed, table = pl.pallas_call(
        functools.partial(pack_kernel, azi_count, blocks.shape[0]),
        out_shape=[pltpu.VMEM(shape, F32)] * azi_count
        + [jax.ShapeDtypeStruct((spots + 1,), jnp.int32)],
        in_specs=[SMEM, HBM],
        out_specs=[VMEM] * azi_count + [SMEM],
        scratch_shapes=[
            pltpu.SMEM((spots,), jnp.int32),
            pltpu.SMEM((azi_count,), jnp.int32),
            pltpu.SemaphoreType.DMA((spots,)),
        ],
        compiler_params=pltpu.CompilerParams(vmem_limit_bytes=4 * MIB),
        name="pack",
    )(assignment, pltpu.with_memory_space_constraint(blocks, pltpu.HBM))
    return packed, table


def coefficients(block_count, levels, damping, coupling, weights, ratio, relax):
    group = lane_group()
    for d in range(3):
        weights[:, d * CHANNELS : (d + 1) * CHANNELS] = 0.5 * coupling[d]
    for half in range(block_count // 8):
        factor = jnp.zeros((CHANNELS, LANES), F32)
        for i in range(8):
            level = levels[half * 8 + i]
            scale = jnp.where(level == 0, 1.0, jnp.where(level == 1, 2.0, 4.0)) * time_step
            factor = jnp.where(group == i, scale, factor)
        ratio[:, half * LANES : (half + 1) * LANES] = factor
    channel = lax.broadcasted_iota(jnp.int32, relax.shape, 0)
    pull = jnp.zeros(relax.shape, F32)
    for c in range(CHANNELS):
        pull = jnp.where(channel == c, time_step * damping[c], pull)
    relax[...] = pull


def order_of(azi_count):
    return [0] + sorted(range(1, azi_count), key=lambda d: abs(2 * d - azi_count))


def unpack_kernel(azi_count, block_count, table, levels, damping, coupling, *refs):
    arrived = {d: refs[i] for i, d in enumerate(order_of(azi_count))}
    field, rad_head, rad_tail, azi_head, azi_tail, sums, held, weights, ratio, relax, sems = refs[
        azi_count:
    ]

    def copy_of(shift, k):
        spot = shift * CAPACITY + k
        slot = jnp.maximum(table[spot], 0)
        return pltpu.make_async_copy(arrived[shift].at[k], held.at[slot], sems.at[spot])

    spots = [(shift, k) for shift in range(azi_count) for k in range(CAPACITY)]
    for shift, k in spots:

        @pl.when(table[shift * CAPACITY + k] >= 0)
        def _(shift=shift, k=k):
            copy_of(shift, k).start()

    coefficients(block_count, levels, damping, coupling, weights, ratio, relax)
    for shift, k in spots:

        @pl.when(table[shift * CAPACITY + k] >= 0)
        def _(shift=shift, k=k):
            copy_of(shift, k).wait()

    group = lane_group()

    def row(x, carry):
        base = x * (EDGE * EDGE)
        for half in range(block_count // 8):
            lanes = slice(half * LANES, (half + 1) * LANES)
            running = None
            for upper in range(2):
                at = pl.ds(pl.multiple_of(base + upper * LANES, LANES), LANES)
                tiles = swap_groups([held[half * 8 + i, :, at] for i in range(8)], group)
                for i in range(8):
                    field[x, upper * 8 + i, :, lanes] = tiles[i]
                    running = tiles[i] if running is None else running + tiles[i]
                for i in range(2):
                    if upper == 0:
                        azi_head[x, i, :, lanes] = tiles[i]
                    else:
                        azi_tail[x, i, :, lanes] = tiles[6 + i]
            sums[x, :, lanes] = running
        return carry

    lax.fori_loop(0, EDGE, row, 0, unroll=2)
    rad_head[...] = field[0:2]
    rad_tail[...] = field[EDGE - 2 : EDGE]


def field_shapes(vertical):
    rad = pltpu.VMEM((2, EDGE, CHANNELS, vertical), F32)
    azi = pltpu.VMEM((EDGE, 2, CHANNELS, vertical), F32)
    field = pltpu.VMEM((EDGE, EDGE, CHANNELS, vertical), F32)
    return [field, rad, rad, azi, azi, pltpu.VMEM((EDGE, CHANNELS, vertical), F32)]


def unpack(table, levels, damping, coupling, arrived, block_shape):
    azi_count = len(arrived)
    vertical = block_shape[0] * EDGE
    return pl.pallas_call(
        functools.partial(unpack_kernel, azi_count, block_shape[0]),
        out_shape=field_shapes(vertical)
        + [
            pltpu.VMEM(block_shape, F32),
            pltpu.VMEM((CHANNELS, 3 * CHANNELS), F32),
            pltpu.VMEM((CHANNELS, vertical), F32),
            pltpu.VMEM((CHANNELS, vertical), F32),
        ],
        in_specs=[SMEM, SMEM, SMEM, VMEM] + [ANY] * azi_count,
        out_specs=[VMEM] * 10,
        scratch_shapes=[pltpu.SemaphoreType.DMA((azi_count * CAPACITY,))],
        compiler_params=pltpu.CompilerParams(vmem_limit_bytes=16 * MIB),
        name="unpack",
    )(table, levels, damping, coupling, *(arrived[d] for d in order_of(azi_count)))


def shear_of(x):
    cell = (lax.axis_index("rad") * EDGE + x).astype(F32)
    return shear_rate * ((cell + 0.5) * (2.0 / (EDGE * lax.axis_size("rad"))) - 1.0)


def mean_of(sums, x):
    return sums[x] * (1.0 / (EDGE * lax.axis_size("azi")))


def start_radius(get, x, y, carry_slope, carry_plus):
    u = [get(x + i, y) for i in (-2, -1, 0, 1)]
    e = [u[i + 1] - u[i] for i in range(3)]
    before, slope = minmod(e[0], e[1]), minmod(e[1], e[2])
    carry_slope[y] = slope
    carry_plus[y] = e[1] + 0.5 * (slope - before)


def stage_row(get, x, cells, carry_slope, carry_plus, left, step, pull, outs):
    settled, sums_azi, jumps_azi = outs
    low = cells[0]
    u = [get(x, low + i) for i in (-2, -1, 0, 1)]
    vertical = u[0].shape[-1]
    e = [u[i + 1] - u[i] for i in range(3)]
    before, slope = minmod(e[0], e[1]), minmod(e[1], e[2])
    plus = e[1] + 0.5 * (slope - before)
    cell, upper, face = u[2], u[3], e[2]
    for y in cells:
        beyond = get(x, y + 2)
        face_next = beyond - upper
        slope_next = minmod(face, face_next)
        k = 0.5 * (slope_next - slope)
        minus = face - k
        sum_azi = plus + minus
        jump_azi = minus - plus
        plus = face + k
        slope, face = slope_next, face_next
        r1, r2 = get(x + 1, y), get(x + 2, y)
        e1 = r1 - cell
        s1 = minmod(e1, r2 - r1)
        k = 0.5 * (s1 - carry_slope[y])
        minus = e1 - k
        before = carry_plus[y]
        sum_rad = before + minus
        jump = minus - before
        carry_plus[y] = e1 + k
        carry_slope[y] = s1
        f1 = pltpu.roll(cell, vertical - 1, 1) - cell
        g1 = minmod(pltpu.roll(f1, 1, 1), f1)
        k = 0.5 * (pltpu.roll(g1, vertical - 1, 1) - g1)
        minus = f1 - k
        before = pltpu.roll(f1 + k, 1, 1)
        sum_vert = before + minus
        jump = jump + (minus - before)
        stack = []
        for part in (sum_rad, sum_azi, sum_vert):
            high = part.astype(jnp.bfloat16).astype(F32)
            stack += [high, part - high]
        stack = jnp.concatenate(stack, axis=0).astype(jnp.bfloat16)
        pair = lax.dot_general(left, stack, (((1,), (0,)), ((), ())), preferred_element_type=F32)
        flux = (pair[:CHANNELS] + pair[CHANNELS:]) - jump
        settled[x, y] = cell - step * flux - pull * cell
        sums_azi[x, y] = step * sum_azi
        jumps_azi[x, y] = step * jump_azi
        cell, upper = upper, beyond


def split_weights(weights):
    w = weights[...]
    high = w.astype(jnp.bfloat16).astype(F32)
    both = jnp.concatenate([high, w - high], axis=0)
    columns = [both[:, CHANNELS * (i // 2) : CHANNELS * (i // 2 + 1)] for i in range(6)]
    return jnp.concatenate(columns, axis=1).astype(jnp.bfloat16)


def sweep(get, rows, runs, carry_slope, carry_plus, left, ratio, relax, outs, unroll=1):
    for cells in runs:
        for y in cells:
            start_radius(get, rows[0], y, carry_slope, carry_plus)

    def row(x, carry):
        for cells in runs:
            stage_row(
                get, x, cells, carry_slope, carry_plus, left, ratio[...], relax[...], outs
            )
        return carry

    lax.fori_loop(rows[0], rows[1], row, 0, unroll=unroll)


INNER = range(2, EDGE - 2)
HEAD, TAIL = range(0, 2), range(EDGE - 2, EDGE)


def inner_kernel(field, weights, ratio, relax, *refs):
    outs, carries = refs[:3], refs[3:]

    def get(x, y):
        return field[x, y]

    sweep(get, (2, EDGE - 2), (INNER,), *carries, split_weights(weights), ratio, relax, outs, unroll=4)


def inner_stage(field, weights, ratio, relax):
    vertical = field.shape[-1]
    return pl.pallas_call(
        inner_kernel,
        out_shape=[pltpu.VMEM(field.shape, F32)] * 3,
        in_specs=[VMEM] * 4,
        out_specs=[VMEM] * 3,
        scratch_shapes=[pltpu.VMEM((EDGE, CHANNELS, vertical), F32)] * 2,
        compiler_params=pltpu.CompilerParams(vmem_limit_bytes=16 * MIB),
        cost_estimate=COST,
        name="inner_stage",
    )(field, weights, ratio, relax)


def outer_kernel(
    field, low_azi, low_rad, high_azi, high_rad, weights, ratio, relax, one, two, three, *refs
):
    del one, two, three
    outs = refs[:3]
    padded, carry_slope, carry_plus, sems = refs[3:]
    load_padded(field, low_rad, high_rad, low_azi, high_azi, padded, sems)

    def get(x, y):
        return padded[x + 2, y + 2]

    rest = (carry_slope, carry_plus, split_weights(weights), ratio, relax, outs)
    sweep(get, (0, 2), (range(EDGE),), *rest)
    sweep(get, (2, EDGE - 2), (HEAD, TAIL), *rest, unroll=12)
    sweep(get, (EDGE - 2, EDGE), (range(EDGE),), *rest)


def outer_stage(field, halos, weights, ratio, relax, parts):
    vertical = field.shape[-1]
    return pl.pallas_call(
        outer_kernel,
        out_shape=[pltpu.VMEM(field.shape, F32)] * 3,
        in_specs=[ANY] * 5 + [VMEM] * 6,
        out_specs=[VMEM] * 3,
        scratch_shapes=[
            pltpu.VMEM((EDGE + 4, EDGE + 4, CHANNELS, vertical), F32),
            pltpu.VMEM((EDGE, CHANNELS, vertical), F32),
            pltpu.VMEM((EDGE, CHANNELS, vertical), F32),
            pltpu.SemaphoreType.DMA((5,)),
        ],
        input_output_aliases={8: 0, 9: 1, 10: 2},
        compiler_params=pltpu.CompilerParams(vmem_limit_bytes=16 * MIB),
        cost_estimate=COST,
        name="outer_stage",
    )(field, *halos, weights, ratio, relax, *parts)


def speeds(average, x):
    velocity = jnp.broadcast_to(average[2:3, :], average.shape) + shear_of(x)
    return 0.5 * velocity, 0.5 * jnp.abs(velocity) + 0.5 * signal_speed


def split_weights(weights):
    w = weights[...]
    high = w.astype(jnp.bfloat16).astype(F32)
    both = jnp.concatenate([high, w - high], axis=0)
    columns = [both[:, CHANNELS * (i // 2) : CHANNELS * (i // 2 + 1)] for i in range(6)]
    return jnp.concatenate(columns, axis=1).astype(jnp.bfloat16)


def load_padded(field, low_rad, high_rad, low_azi, high_azi, padded, sems):
    middle = pl.ds(2, EDGE)
    copies = [
        (field, padded.at[middle, middle]),
        (low_rad, padded.at[pl.ds(0, 2), middle]),
        (high_rad, padded.at[pl.ds(EDGE + 2, 2), middle]),
        (low_azi, padded.at[middle, pl.ds(0, 2)]),
        (high_azi, padded.at[middle, pl.ds(EDGE + 2, 2)]),
    ]
    copies = [pltpu.make_async_copy(a, b, sems.at[i]) for i, (a, b) in enumerate(copies)]
    for copy in copies:
        copy.start()
    for copy in copies:
        copy.wait()


def join_kernel(
    settled, sums_azi, jumps_azi, column, relax,
    state, rad_head, rad_tail, azi_head, azi_tail, sums,
):
    def row(x, carry):
        average = mean_of(column, x)
        half_velocity, half_signal = speeds(average, x)
        pulled = relax[...] * average
        running = None
        for y in range(EDGE):
            value = (
                (settled[x, y] + pulled)
                - half_velocity * sums_azi[x, y]
                + half_signal * jumps_azi[x, y]
            )
            state[x, y] = value
            if y < 2:
                azi_head[x, y] = value
            if y >= EDGE - 2:
                azi_tail[x, y - (EDGE - 2)] = value
            running = value if running is None else running + value
        sums[x] = running
        return carry

    lax.fori_loop(0, EDGE, row, 0)
    rad_head[...] = state[0:2]
    rad_tail[...] = state[EDGE - 2 : EDGE]


def join_stage(parts, column, relax):
    vertical = parts[0].shape[-1]
    return pl.pallas_call(
        join_kernel,
        out_shape=field_shapes(vertical),
        in_specs=[VMEM] * 5,
        out_specs=[VMEM] * 6,
        compiler_params=pltpu.CompilerParams(vmem_limit_bytes=8 * MIB),
        name="join_stage",
    )(*parts, column, relax)


def final_kernel(
    held, settled, sums_azi, jumps_azi, column, relax,
    final, tendency, final_rows, tendency_rows, out_sems,
):
    group = lane_group()
    halves = held.shape[0] // 8

    def out_copies(x):
        at = pl.ds(pl.multiple_of(x * (EDGE * EDGE), LANES), EDGE * EDGE)
        return [
            pltpu.make_async_copy(a.at[:, :, at], b.at[:, :, at], out_sems.at[i, x])
            for i, (a, b) in enumerate(((final_rows, final), (tendency_rows, tendency)))
        ]

    def row(x, carry):
        average = mean_of(column, x)
        half_velocity, half_signal = speeds(average, x)
        pulled = relax[...] * average
        base = x * (EDGE * EDGE)
        for half in range(halves):
            lanes = slice(half * LANES, (half + 1) * LANES)
            for upper in range(2):
                at = pl.ds(pl.multiple_of(base + upper * LANES, LANES), LANES)
                results = []
                for i in range(8):
                    y = upper * 8 + i
                    results.append(
                        (settled[x, y, :, lanes] + pulled[:, lanes])
                        - half_velocity[:, lanes] * sums_azi[x, y, :, lanes]
                        + half_signal[:, lanes] * jumps_azi[x, y, :, lanes]
                    )
                for i, tile in enumerate(swap_groups(results, group)):
                    start = held[half * 8 + i, :, at]
                    change = 0.5 * (tile - start)
                    final_rows[half * 8 + i, :, at] = start + change
                    tendency_rows[half * 8 + i, :, at] = change * (1.0 / time_step)
        for copy in out_copies(x):
            copy.start()
        return carry

    lax.fori_loop(0, EDGE, row, 0, unroll=2)

    def finish_row(x, carry):
        for copy in out_copies(x):
            copy.wait()
        return carry

    lax.fori_loop(0, EDGE, finish_row, 0)


def final_stage(held, parts, column, relax):
    return pl.pallas_call(
        final_kernel,
        out_shape=[jax.ShapeDtypeStruct(held.shape, F32)] * 2,
        in_specs=[VMEM] * 6,
        out_specs=[HBM] * 2,
        scratch_shapes=[
            pltpu.VMEM(held.shape, F32),
            pltpu.VMEM(held.shape, F32),
            pltpu.SemaphoreType.DMA((2, EDGE)),
        ],
        compiler_params=pltpu.CompilerParams(vmem_limit_bytes=8 * MIB),
        name="final_stage",
    )(held, *parts, column, relax)


def sum_azi(values, beside):
    count = lax.axis_size("azi")
    if count & (count - 1):
        return lax.psum(values, "azi"), beside
    step = 1
    while step < count:
        other = lax.ppermute(values, "azi", [(i, i ^ step) for i in range(count)])
        if step == 2:
            other, beside = lax.optimization_barrier((other, beside))
        values = values + other
        step *= 2
    return values, beside


def exchange(rad_head, rad_tail, azi_head, azi_tail):
    rad, azi = lax.axis_size("rad"), lax.axis_size("azi")
    return (
        lax.ppermute(azi_tail, "azi", [(i, (i + 1) % azi) for i in range(azi)]),
        lax.ppermute(rad_tail, "rad", [(i, i + 1) for i in range(rad - 1)]),
        lax.ppermute(azi_head, "azi", [((i + 1) % azi, i) for i in range(azi)]),
        lax.ppermute(rad_head, "rad", [(i + 1, i) for i in range(rad - 1)]),
    )


def on_device(blocks, assignment, levels, coupling, damping):
    azi_count = lax.axis_size("azi")
    packed, table = pack(assignment, blocks, azi_count)
    arrived = [packed[0]] + [
        lax.ppermute(packed[d], "azi", [(i, (i + d) % azi_count) for i in range(azi_count)])
        for d in range(1, azi_count)
    ]
    start, *edges, sums, held, weights, ratio, relax = unpack(
        table, levels, damping, coupling, arrived, blocks.shape
    )

    def section(field, edges, sums):
        halos = exchange(*edges)
        parts = inner_stage(field, weights, ratio, relax)
        column, parts = sum_azi(sums, parts)
        return outer_stage(field, halos, weights, ratio, relax, parts), column

    parts, column = section(start, edges, sums)
    state, *edges, sums = join_stage(parts, column, relax)
    parts, column = section(state, edges, sums)
    return final_stage(held, parts, column, relax)


def solution(mesh):
    in_specs = (P(("rad", "azi"), None, None), P(), P(("rad", "azi")), P(), P())
    out_specs = (P(("rad", "azi"), None, None), P(("rad", "azi"), None, None))
    return jax.shard_map(
        on_device, mesh=mesh, in_specs=in_specs, out_specs=out_specs, check_vma=False
    )
```

```python
import functools

import jax
import jax.numpy as jnp
from jax import lax
from jax.experimental import pallas as pl
from jax.experimental.pallas import tpu as pltpu
from jax.sharding import PartitionSpec as P

EDGE = 16
CHANNELS = 8
CAPACITY = 2
LANES = 128

time_step = 0.02
signal_speed = 2.0
shear_rate = -1.5

ANY = pl.BlockSpec(memory_space=pl.ANY)
SMEM = pl.BlockSpec(memory_space=pltpu.SMEM)
HBM = pl.BlockSpec(memory_space=pltpu.HBM)
VMEM = pl.BlockSpec(memory_space=pltpu.VMEM)
MIB = 1 << 20
COST = pl.CostEstimate(flops=0, bytes_accessed=0, transcendentals=0)
F32 = jnp.float32


def minmod(a, b):
    return jnp.maximum(jnp.minimum(a, b), jnp.minimum(jnp.maximum(a, b), 0.0))


def lane_group():
    return lax.broadcasted_iota(jnp.int32, (CHANNELS, LANES), 1) // EDGE


def swap_groups(rows, group):
    rows = list(rows)
    for bit in (1, 2, 4):
        low = (group & bit) == 0
        shift = EDGE * bit
        for i in range(8):
            if i & bit:
                continue
            a, b = rows[i], rows[i + bit]
            rows[i] = jnp.where(low, a, pltpu.roll(b, shift, 1))
            rows[i + bit] = jnp.where(low, pltpu.roll(a, LANES - shift, 1), b)
    return rows


def own_place():
    azi_count = lax.axis_size("azi")
    azi = lax.axis_index("azi")
    return azi, lax.axis_index("rad") * azi_count + azi


def pack_kernel(azi_count, block_count, assignment, blocks, *refs):
    outs = refs[:azi_count]
    table, sent, fill, sems = refs[azi_count:]
    azi, own = own_place()
    first = own * block_count
    row_first = (own - azi) * block_count
    spots = azi_count * CAPACITY
    for i in range(azi_count):
        fill[i] = 0
    for i in range(spots):
        sent[i] = 0
        table[i] = -1

    def note(j, carry):
        device = lax.div(assignment[first + j], block_count)
        shift = lax.rem(lax.rem(device, azi_count) - azi + azi_count, azi_count)
        k = fill[shift]
        sent[shift * CAPACITY + k] = j
        fill[shift] = k + 1
        return carry

    lax.fori_loop(0, block_count, note, 0, unroll=True)
    copies = []
    for shift in range(azi_count):
        for k in range(CAPACITY):
            spot = shift * CAPACITY + k
            copy = pltpu.make_async_copy(blocks.at[sent[spot]], outs[shift].at[k], sems.at[spot])
            copy.start()
            copies.append(copy)

    def source(s, carry):
        shift = lax.rem(azi - s + azi_count, azi_count)
        start = row_first + s * block_count
        found = jnp.int32(0)
        for j in range(block_count):
            slot = assignment[start + j] - first
            ours = (slot >= 0) & (slot < block_count)
            table[jnp.where(ours, shift * CAPACITY + found, spots)] = slot
            found = found + ours.astype(jnp.int32)
        return carry

    lax.fori_loop(0, azi_count, source, 0)
    for copy in copies:
        copy.wait()


def pack(assignment, blocks, azi_count):
    shape = (CAPACITY,) + blocks.shape[1:]
    spots = azi_count * CAPACITY
    *packed, table = pl.pallas_call(
        functools.partial(pack_kernel, azi_count, blocks.shape[0]),
        out_shape=[pltpu.VMEM(shape, F32)] * azi_count
        + [jax.ShapeDtypeStruct((spots + 1,), jnp.int32)],
        in_specs=[SMEM, HBM],
        out_specs=[VMEM] * azi_count + [SMEM],
        scratch_shapes=[
            pltpu.SMEM((spots,), jnp.int32),
            pltpu.SMEM((azi_count,), jnp.int32),
            pltpu.SemaphoreType.DMA((spots,)),
        ],
        compiler_params=pltpu.CompilerParams(vmem_limit_bytes=4 * MIB),
        name="pack",
    )(assignment, pltpu.with_memory_space_constraint(blocks, pltpu.HBM))
    return packed, table


def coefficients(block_count, levels, damping, coupling, weights, ratio, relax):
    group = lane_group()
    for d in range(3):
        weights[:, d * CHANNELS : (d + 1) * CHANNELS] = 0.5 * coupling[d]
    for half in range(block_count // 8):
        factor = jnp.zeros((CHANNELS, LANES), F32)
        for i in range(8):
            level = levels[half * 8 + i]
            scale = jnp.where(level == 0, 1.0, jnp.where(level == 1, 2.0, 4.0)) * time_step
            factor = jnp.where(group == i, scale, factor)
        ratio[:, half * LANES : (half + 1) * LANES] = factor
    channel = lax.broadcasted_iota(jnp.int32, relax.shape, 0)
    pull = jnp.zeros(relax.shape, F32)
    for c in range(CHANNELS):
        pull = jnp.where(channel == c, time_step * damping[c], pull)
    relax[...] = pull


def order_of(azi_count):
    return [0] + sorted(range(1, azi_count), key=lambda d: abs(2 * d - azi_count))


def unpack_kernel(azi_count, block_count, table, levels, damping, coupling, *refs):
    arrived = {d: refs[i] for i, d in enumerate(order_of(azi_count))}
    field, rad_head, rad_tail, azi_head, azi_tail, sums, held, weights, ratio, relax, sems = refs[
        azi_count:
    ]

    def copy_of(shift, k):
        spot = shift * CAPACITY + k
        slot = jnp.maximum(table[spot], 0)
        return pltpu.make_async_copy(arrived[shift].at[k], held.at[slot], sems.at[spot])

    spots = [(shift, k) for shift in range(azi_count) for k in range(CAPACITY)]
    for shift, k in spots:

        @pl.when(table[shift * CAPACITY + k] >= 0)
        def _(shift=shift, k=k):
            copy_of(shift, k).start()

    coefficients(block_count, levels, damping, coupling, weights, ratio, relax)
    for shift, k in spots:

        @pl.when(table[shift * CAPACITY + k] >= 0)
        def _(shift=shift, k=k):
            copy_of(shift, k).wait()

    group = lane_group()

    def row(x, carry):
        base = x * (EDGE * EDGE)
        for half in range(block_count // 8):
            lanes = slice(half * LANES, (half + 1) * LANES)
            running = None
            for upper in range(2):
                at = pl.ds(pl.multiple_of(base + upper * LANES, LANES), LANES)
                tiles = swap_groups([held[half * 8 + i, :, at] for i in range(8)], group)
                for i in range(8):
                    field[x, upper * 8 + i, :, lanes] = tiles[i]
                    running = tiles[i] if running is None else running + tiles[i]
                for i in range(2):
                    if upper == 0:
                        azi_head[x, i, :, lanes] = tiles[i]
                    else:
                        azi_tail[x, i, :, lanes] = tiles[6 + i]
            sums[x, :, lanes] = running
        return carry

    lax.fori_loop(0, EDGE, row, 0, unroll=2)
    rad_head[...] = field[0:2]
    rad_tail[...] = field[EDGE - 2 : EDGE]


def field_shapes(vertical):
    rad = pltpu.VMEM((2, EDGE, CHANNELS, vertical), F32)
    azi = pltpu.VMEM((EDGE, 2, CHANNELS, vertical), F32)
    field = pltpu.VMEM((EDGE, EDGE, CHANNELS, vertical), F32)
    return [field, rad, rad, azi, azi, pltpu.VMEM((EDGE, CHANNELS, vertical), F32)]


def unpack(table, levels, damping, coupling, arrived, block_shape):
    azi_count = len(arrived)
    vertical = block_shape[0] * EDGE
    return pl.pallas_call(
        functools.partial(unpack_kernel, azi_count, block_shape[0]),
        out_shape=field_shapes(vertical)
        + [
            pltpu.VMEM(block_shape, F32),
            pltpu.VMEM((CHANNELS, 3 * CHANNELS), F32),
            pltpu.VMEM((CHANNELS, vertical), F32),
            pltpu.VMEM((CHANNELS, vertical), F32),
        ],
        in_specs=[SMEM, SMEM, SMEM, VMEM] + [ANY] * azi_count,
        out_specs=[VMEM] * 10,
        scratch_shapes=[pltpu.SemaphoreType.DMA((azi_count * CAPACITY,))],
        compiler_params=pltpu.CompilerParams(vmem_limit_bytes=16 * MIB),
        name="unpack",
    )(table, levels, damping, coupling, *(arrived[d] for d in order_of(azi_count)))


def shear_of(x):
    cell = (lax.axis_index("rad") * EDGE + x).astype(F32)
    return shear_rate * ((cell + 0.5) * (2.0 / (EDGE * lax.axis_size("rad"))) - 1.0)


def mean_of(sums, x):
    return sums[x] * (1.0 / (EDGE * lax.axis_size("azi")))


def start_radius(get, x, y, carry_slope, carry_plus):
    u = [get(x + i, y) for i in (-2, -1, 0, 1)]
    e = [u[i + 1] - u[i] for i in range(3)]
    before, slope = minmod(e[0], e[1]), minmod(e[1], e[2])
    carry_slope[y] = slope
    carry_plus[y] = e[1] + 0.5 * (slope - before)


def stage_row(get, x, cells, carry_slope, carry_plus, left, step, pull, outs):
    settled, sums_azi, jumps_azi = outs
    low = cells[0]
    u = [get(x, low + i) for i in (-2, -1, 0, 1)]
    vertical = u[0].shape[-1]
    e = [u[i + 1] - u[i] for i in range(3)]
    before, slope = minmod(e[0], e[1]), minmod(e[1], e[2])
    plus = e[1] + 0.5 * (slope - before)
    cell, upper, face = u[2], u[3], e[2]
    for y in cells:
        beyond = get(x, y + 2)
        face_next = beyond - upper
        slope_next = minmod(face, face_next)
        k = 0.5 * (slope_next - slope)
        minus = face - k
        sum_azi = plus + minus
        jump_azi = minus - plus
        plus = face + k
        slope, face = slope_next, face_next
        r1, r2 = get(x + 1, y), get(x + 2, y)
        e1 = r1 - cell
        s1 = minmod(e1, r2 - r1)
        k = 0.5 * (s1 - carry_slope[y])
        minus = e1 - k
        before = carry_plus[y]
        sum_rad = before + minus
        jump = minus - before
        carry_plus[y] = e1 + k
        carry_slope[y] = s1
        f1 = pltpu.roll(cell, vertical - 1, 1) - cell
        g1 = minmod(pltpu.roll(f1, 1, 1), f1)
        k = 0.5 * (pltpu.roll(g1, vertical - 1, 1) - g1)
        minus = f1 - k
        before = pltpu.roll(f1 + k, 1, 1)
        sum_vert = before + minus
        jump = jump + (minus - before)
        stack = []
        for part in (sum_rad, sum_azi, sum_vert):
            high = part.astype(jnp.bfloat16).astype(F32)
            stack += [high, part - high]
        stack = jnp.concatenate(stack, axis=0).astype(jnp.bfloat16)
        pair = lax.dot_general(left, stack, (((1,), (0,)), ((), ())), preferred_element_type=F32)
        flux = (pair[:CHANNELS] + pair[CHANNELS:]) - jump
        settled[x, y] = cell - step * flux - pull * cell
        sums_azi[x, y] = step * sum_azi
        jumps_azi[x, y] = step * jump_azi
        cell, upper = upper, beyond


def split_weights(weights):
    w = weights[...]
    high = w.astype(jnp.bfloat16).astype(F32)
    both = jnp.concatenate([high, w - high], axis=0)
    columns = [both[:, CHANNELS * (i // 2) : CHANNELS * (i // 2 + 1)] for i in range(6)]
    return jnp.concatenate(columns, axis=1).astype(jnp.bfloat16)


def sweep(get, rows, runs, carry_slope, carry_plus, left, ratio, relax, outs, unroll=1):
    for cells in runs:
        for y in cells:
            start_radius(get, rows[0], y, carry_slope, carry_plus)

    def row(x, carry):
        for cells in runs:
            stage_row(
                get, x, cells, carry_slope, carry_plus, left, ratio[...], relax[...], outs
            )
        return carry

    lax.fori_loop(rows[0], rows[1], row, 0, unroll=unroll)


INNER = range(2, EDGE - 2)
HEAD, TAIL = range(0, 2), range(EDGE - 2, EDGE)


def inner_kernel(field, weights, ratio, relax, *refs):
    outs, carries = refs[:3], refs[3:]

    def get(x, y):
        return field[x, y]

    sweep(get, (2, EDGE - 2), (INNER,), *carries, split_weights(weights), ratio, relax, outs, unroll=4)


def inner_stage(field, weights, ratio, relax):
    vertical = field.shape[-1]
    return pl.pallas_call(
        inner_kernel,
        out_shape=[pltpu.VMEM(field.shape, F32)] * 3,
        in_specs=[VMEM] * 4,
        out_specs=[VMEM] * 3,
        scratch_shapes=[pltpu.VMEM((EDGE, CHANNELS, vertical), F32)] * 2,
        compiler_params=pltpu.CompilerParams(vmem_limit_bytes=16 * MIB),
        cost_estimate=COST,
        name="inner_stage",
    )(field, weights, ratio, relax)


def outer_kernel(
    field, low_azi, low_rad, high_azi, high_rad, weights, ratio, relax, one, two, three, *refs
):
    del one, two, three
    outs = refs[:3]
    padded, carry_slope, carry_plus, sems = refs[3:]
    load_padded(field, low_rad, high_rad, low_azi, high_azi, padded, sems)

    def get(x, y):
        return padded[x + 2, y + 2]

    rest = (carry_slope, carry_plus, split_weights(weights), ratio, relax, outs)
    sweep(get, (0, 2), (range(EDGE // 2), range(EDGE // 2, EDGE)), *rest)
    sweep(get, (2, EDGE - 2), (HEAD, TAIL), *rest, unroll=12)
    sweep(get, (EDGE - 2, EDGE), (range(EDGE // 2), range(EDGE // 2, EDGE)), *rest)


def outer_stage(field, halos, weights, ratio, relax, parts):
    vertical = field.shape[-1]
    return pl.pallas_call(
        outer_kernel,
        out_shape=[pltpu.VMEM(field.shape, F32)] * 3,
        in_specs=[ANY] * 5 + [VMEM] * 6,
        out_specs=[VMEM] * 3,
        scratch_shapes=[
            pltpu.VMEM((EDGE + 4, EDGE + 4, CHANNELS, vertical), F32),
            pltpu.VMEM((EDGE, CHANNELS, vertical), F32),
            pltpu.VMEM((EDGE, CHANNELS, vertical), F32),
            pltpu.SemaphoreType.DMA((5,)),
        ],
        input_output_aliases={8: 0, 9: 1, 10: 2},
        compiler_params=pltpu.CompilerParams(vmem_limit_bytes=16 * MIB),
        cost_estimate=COST,
        name="outer_stage",
    )(field, *halos, weights, ratio, relax, *parts)


def speeds(average, x):
    velocity = jnp.broadcast_to(average[2:3, :], average.shape) + shear_of(x)
    return 0.5 * velocity, 0.5 * jnp.abs(velocity) + 0.5 * signal_speed


def split_weights(weights):
    w = weights[...]
    high = w.astype(jnp.bfloat16).astype(F32)
    both = jnp.concatenate([high, w - high], axis=0)
    columns = [both[:, CHANNELS * (i // 2) : CHANNELS * (i // 2 + 1)] for i in range(6)]
    return jnp.concatenate(columns, axis=1).astype(jnp.bfloat16)


def load_padded(field, low_rad, high_rad, low_azi, high_azi, padded, sems):
    middle = pl.ds(2, EDGE)
    copies = [
        (field, padded.at[middle, middle]),
        (low_rad, padded.at[pl.ds(0, 2), middle]),
        (high_rad, padded.at[pl.ds(EDGE + 2, 2), middle]),
        (low_azi, padded.at[middle, pl.ds(0, 2)]),
        (high_azi, padded.at[middle, pl.ds(EDGE + 2, 2)]),
    ]
    copies = [pltpu.make_async_copy(a, b, sems.at[i]) for i, (a, b) in enumerate(copies)]
    for copy in copies:
        copy.start()
    for copy in copies:
        copy.wait()


def join_kernel(
    settled, sums_azi, jumps_azi, column, relax,
    state, rad_head, rad_tail, azi_head, azi_tail, sums,
):
    def row(x, carry):
        average = mean_of(column, x)
        half_velocity, half_signal = speeds(average, x)
        pulled = relax[...] * average
        running = None
        for y in range(EDGE):
            value = (
                (settled[x, y] + pulled)
                - half_velocity * sums_azi[x, y]
                + half_signal * jumps_azi[x, y]
            )
            state[x, y] = value
            if y < 2:
                azi_head[x, y] = value
            if y >= EDGE - 2:
                azi_tail[x, y - (EDGE - 2)] = value
            running = value if running is None else running + value
        sums[x] = running
        return carry

    lax.fori_loop(0, EDGE, row, 0)
    rad_head[...] = state[0:2]
    rad_tail[...] = state[EDGE - 2 : EDGE]


def join_stage(parts, column, relax):
    vertical = parts[0].shape[-1]
    return pl.pallas_call(
        join_kernel,
        out_shape=field_shapes(vertical),
        in_specs=[VMEM] * 5,
        out_specs=[VMEM] * 6,
        compiler_params=pltpu.CompilerParams(vmem_limit_bytes=8 * MIB),
        name="join_stage",
    )(*parts, column, relax)


def final_kernel(
    held, settled, sums_azi, jumps_azi, column, relax,
    final, tendency, final_rows, tendency_rows, out_sems,
):
    group = lane_group()
    halves = held.shape[0] // 8

    def out_copies(x):
        at = pl.ds(pl.multiple_of(x * (EDGE * EDGE), LANES), EDGE * EDGE)
        return [
            pltpu.make_async_copy(a.at[:, :, at], b.at[:, :, at], out_sems.at[i, x])
            for i, (a, b) in enumerate(((final_rows, final), (tendency_rows, tendency)))
        ]

    def row(x, carry):
        average = mean_of(column, x)
        half_velocity, half_signal = speeds(average, x)
        pulled = relax[...] * average
        base = x * (EDGE * EDGE)
        for half in range(halves):
            lanes = slice(half * LANES, (half + 1) * LANES)
            for upper in range(2):
                at = pl.ds(pl.multiple_of(base + upper * LANES, LANES), LANES)
                results = []
                for i in range(8):
                    y = upper * 8 + i
                    results.append(
                        (settled[x, y, :, lanes] + pulled[:, lanes])
                        - half_velocity[:, lanes] * sums_azi[x, y, :, lanes]
                        + half_signal[:, lanes] * jumps_azi[x, y, :, lanes]
                    )
                for i, tile in enumerate(swap_groups(results, group)):
                    start = held[half * 8 + i, :, at]
                    change = 0.5 * (tile - start)
                    final_rows[half * 8 + i, :, at] = start + change
                    tendency_rows[half * 8 + i, :, at] = change * (1.0 / time_step)
        for copy in out_copies(x):
            copy.start()
        return carry

    lax.fori_loop(0, EDGE, row, 0, unroll=2)

    def finish_row(x, carry):
        for copy in out_copies(x):
            copy.wait()
        return carry

    lax.fori_loop(0, EDGE, finish_row, 0)


def final_stage(held, parts, column, relax):
    return pl.pallas_call(
        final_kernel,
        out_shape=[jax.ShapeDtypeStruct(held.shape, F32)] * 2,
        in_specs=[VMEM] * 6,
        out_specs=[HBM] * 2,
        scratch_shapes=[
            pltpu.VMEM(held.shape, F32),
            pltpu.VMEM(held.shape, F32),
            pltpu.SemaphoreType.DMA((2, EDGE)),
        ],
        compiler_params=pltpu.CompilerParams(vmem_limit_bytes=8 * MIB),
        name="final_stage",
    )(held, *parts, column, relax)


def sum_azi(values, beside):
    count = lax.axis_size("azi")
    if count & (count - 1):
        return lax.psum(values, "azi"), beside
    step = 1
    while step < count:
        other = lax.ppermute(values, "azi", [(i, i ^ step) for i in range(count)])
        if step == 2:
            other, beside = lax.optimization_barrier((other, beside))
        values = values + other
        step *= 2
    return values, beside


def exchange(rad_head, rad_tail, azi_head, azi_tail):
    rad, azi = lax.axis_size("rad"), lax.axis_size("azi")
    return (
        lax.ppermute(azi_tail, "azi", [(i, (i + 1) % azi) for i in range(azi)]),
        lax.ppermute(rad_tail, "rad", [(i, i + 1) for i in range(rad - 1)]),
        lax.ppermute(azi_head, "azi", [((i + 1) % azi, i) for i in range(azi)]),
        lax.ppermute(rad_head, "rad", [(i + 1, i) for i in range(rad - 1)]),
    )


def on_device(blocks, assignment, levels, coupling, damping):
    azi_count = lax.axis_size("azi")
    packed, table = pack(assignment, blocks, azi_count)
    arrived = [packed[0]] + [
        lax.ppermute(packed[d], "azi", [(i, (i + d) % azi_count) for i in range(azi_count)])
        for d in range(1, azi_count)
    ]
    start, *edges, sums, held, weights, ratio, relax = unpack(
        table, levels, damping, coupling, arrived, blocks.shape
    )

    def section(field, edges, sums):
        halos = exchange(*edges)
        parts = inner_stage(field, weights, ratio, relax)
        column, parts = sum_azi(sums, parts)
        return outer_stage(field, halos, weights, ratio, relax, parts), column

    parts, column = section(start, edges, sums)
    state, *edges, sums = join_stage(parts, column, relax)
    parts, column = section(state, edges, sums)
    return final_stage(held, parts, column, relax)


def solution(mesh):
    in_specs = (P(("rad", "azi"), None, None), P(), P(("rad", "azi")), P(), P())
    out_specs = (P(("rad", "azi"), None, None), P(("rad", "azi"), None, None))
    return jax.shard_map(
        on_device, mesh=mesh, in_specs=in_specs, out_specs=out_specs, check_vma=False
    )
```
